256 devices in a mesh: row: 16 (over z, core), col: 16 (over x, y).
Axes of the slice: x: 4, y: 4, z: 8, core: 2. Of those that a mesh axis runs over, the one named last changes fastest.
Arguments:
- wrapped_phase: float32 [32768, 8192], P('row', 'col'), may hold values from -2.85 to 2.85, as said below
Outputs:
- unwrapped: float32 [32768, 8192], P('row', 'col')
The draws below stay inside these ranges and needn't reach their ends.
Inputs may be any that keep to these rules, and one draw needn't show every extreme that they name: The difference of wrapped_phase between any two adjacent cells of the map lies 0.14 or more away from every odd multiple of pi.
All inputs are finite; a program needn't handle non-finite values.
Results may differ from the reference program's by a relative error of at most 0.0003.
Values sent between devices are 32-bit elements; how exact they have to be, the bound alone decides.
No kernel may reach another device: no remote copies, remote signals or barrier semaphores. Data moves between devices by JAX's collectives and lax.ppermute only.
A program may use at most 128 MiB of HBM per device.

```python
import math
import jax
import jax.numpy as jnp
from jax import lax

TILE = 256
NX = 32768
NY = 8192


def draw_wrapped_phase(key, part):
    keys = jax.random.split(jax.random.fold_in(key, 11), 5)
    row_index = jnp.arange(NX, dtype=jnp.int32)[:, None]
    col_index = jnp.arange(NY, dtype=jnp.int32)[None, :]
    rates = jax.random.randint(keys[0], (2, 2), 1, 17)
    periods = jax.random.randint(keys[1], (2,), 2, 5)
    anchors = jax.random.randint(keys[2], (2,), 0, 64)
    levels = jnp.zeros((NX, NY), jnp.int32)
    for mode in range(2):
        position = (row_index * rates[mode, 0] + col_index * rates[mode, 1]) // 16 + anchors[mode]
        cycle = jnp.remainder(position, 2 * periods[mode])
        levels = levels + jnp.abs(cycle - periods[mode])
    levels = levels + jax.random.randint(keys[3], (NX, NY), 0, 4)
    centred = jnp.remainder(levels, 7) - 3
    jitter = jax.random.uniform(keys[4], (NX, NY), jnp.float32, -0.149, 0.149)
    return centred.astype(jnp.float32) * (2.0 * math.pi / 7.0) + jitter


def setup_inputs(seed: int = 0) -> dict:
    splits = jax.random.split(jax.random.key(seed), 2)
    wrapped_phase = draw_wrapped_phase(jax.random.fold_in(splits[1], 71), 0)
    return dict(wrapped_phase=wrapped_phase)


HIGHEST = lax.Precision.HIGHEST

def wrap_angle(values):
    return jnp.arctan2(jnp.sin(values), jnp.cos(values))

def cosine_table(length):
    frequency = jnp.arange(length, dtype=jnp.float32)[:, None]
    positions = jnp.arange(length, dtype=jnp.float32)[None, :]
    cosine = jnp.cos(math.pi * frequency * (2.0 * positions + 1.0) / (2.0 * length)) * math.sqrt(2.0 / length)
    return jnp.where(frequency == 0.0, cosine * math.sqrt(0.5), cosine)

def solve_tiles(phase_grid):
    length = phase_grid.shape[1]
    down_slope = wrap_angle(phase_grid[:, 1:] - phase_grid[:, :-1])
    zero_row = jnp.zeros_like(phase_grid[:, :1])
    diverge = jnp.concatenate([down_slope, zero_row], 1) - jnp.concatenate([zero_row, down_slope], 1)
    across = wrap_angle(phase_grid[..., 1:] - phase_grid[..., :-1])
    zero_col = jnp.zeros_like(phase_grid[..., :1])
    diverge = diverge + jnp.concatenate([across, zero_col], 3) - jnp.concatenate([zero_col, across], 3)
    cosine = cosine_table(length)
    spectrum = jnp.einsum('pa,rakb,qb->rpkq', cosine, diverge, cosine, precision=HIGHEST)
    frequency = jnp.arange(length, dtype=jnp.float32)
    wave_cos = 2.0 * jnp.cos(math.pi * frequency / length)
    eigenvalue = wave_cos[:, None] + wave_cos[None, :] - 4.0
    corner = frequency[:, None] + frequency[None, :] == 0.0
    safe_eigen = jnp.where(corner, -1.0, eigenvalue)
    scaled = jnp.where(corner[:, None, :], 0.0, spectrum / safe_eigen[:, None, :])
    return jnp.einsum('pa,rpkq,qb->rakb', cosine, scaled, cosine, precision=HIGHEST)

def reference(wrapped_phase):
    tile_rows = NX // TILE
    tile_cols = NY // TILE
    phase_grid = wrapped_phase.reshape(tile_rows, TILE, tile_cols, TILE)
    solved = lax.map(lambda band_tiles: solve_tiles(band_tiles[None])[0], phase_grid)
    east_jump = lax.optimization_barrier(jnp.mean(solved[:, :, :-1, -1] + wrap_angle(phase_grid[:, :, 1:, 0] - phase_grid[:, :, :-1, -1]) - solved[:, :, 1:, 0], axis=1))
    south_jump = lax.optimization_barrier(jnp.mean(solved[:-1, -1, 0, :] + wrap_angle(phase_grid[1:, 0, 0, :] - phase_grid[:-1, -1, 0, :]) - solved[1:, 0, 0, :], axis=1))
    row_starts = jnp.concatenate([jnp.zeros((1,), jnp.float32), jnp.cumsum(south_jump)])
    along_row = jnp.concatenate([jnp.zeros((tile_rows, 1), jnp.float32), jnp.cumsum(east_jump, axis=1)], 1)
    offsets = row_starts[:, None] + along_row
    return (solved + offsets[:, None, :, None]).reshape(NX, NY)
```

```python
import math

import jax
import jax.numpy as jnp
import ml_dtypes
import numpy as np
from jax import lax
from jax.experimental import pallas as pl
from jax.experimental.pallas import tpu as pltpu
from jax.sharding import PartitionSpec as P

TILE = 256
TURN = 2.0 * math.pi
PER_TURN = 1.0 / TURN
MAGIC = 1.5 * 2.0**23
ROWS = 8
COLS = 2
WIDTH = COLS * TILE
LANES = 128
PARTS = WIDTH // LANES
LOADS = 8
CHUNK = 16
STEPS = TILE // (2 * CHUNK)
MSG = 48
LOW = 4


def split_terms(table, terms):
    parts, rest = [], np.asarray(table, np.float64)
    for _ in range(terms):
        part = rest.astype(ml_dtypes.bfloat16)
        parts.append(part)
        rest = rest - part.astype(np.float64)
    return parts


def tables():
    q = np.arange(TILE, dtype=np.float64)
    c = np.cos(math.pi * q[:, None] * (2.0 * q[None, :] + 1.0) / (2.0 * TILE))
    c *= math.sqrt(2.0 / TILE)
    c[0] *= math.sqrt(0.5)
    forward = np.concatenate(split_terms(c.T, 3), 0)
    high, low = split_terms(TURN * c, 2)
    backward = np.concatenate([high, high, low], 0)
    mu = 4.0 * np.sin(math.pi * q / (2.0 * TILE)) ** 2
    pivot = [1.0 + mu]
    for _ in range(TILE // 2 - 1):
        pivot.append(2.0 + mu - 1.0 / pivot[-1])
    weights = np.stack([1.0 / d for d in pivot])
    last = pivot[-1]
    even = np.zeros_like(mu)
    even[1:] = 0.5 / (last[1:] - 1.0)
    odd = 0.5 / (last + 1.0)
    middle = np.stack([even, odd])
    freq = np.arange(LOW, dtype=np.float32)
    wave = np.float32(2.0) * np.cos(np.float32(math.pi) * freq / np.float32(TILE))
    held = (wave[:, None] + wave[None, :]).astype(np.float32) - np.float32(4.0)
    exact = mu[:LOW, None] + mu[None, :LOW]
    delta = np.zeros((LOW, LOW))
    known = exact > 0.0
    delta[known] = exact[known] / -held[known].astype(np.float64) - 1.0
    lift = np.zeros((2 * LOW, LANES))
    lift[:LOW, :LOW] = delta
    lift[LOW:, :LOW][known] = delta[known] / exact[known]
    basis = np.zeros((TILE, LANES))
    basis[:, :LOW] = c[:LOW].T
    starts = (delta[0, :LOW] * c[:LOW, 0]) @ c[:LOW]
    ends = (delta[0, :LOW] * c[:LOW, -1]) @ c[:LOW]
    after = lambda g: np.cumsum(g[::-1])[::-1] - g
    edges = np.zeros((8, TILE))
    edges[:4] = np.stack([starts, ends, -TURN * after(starts), -TURN * after(ends)]) / TILE
    low = dict(
        lift=lift.astype(np.float32),
        basis=basis.astype(ml_dtypes.bfloat16),
        waves=c[:LOW, : TILE // 2].astype(np.float32).reshape(-1),
        edges=edges.astype(np.float32),
        steps=edges[:4].astype(np.float32).reshape(-1),
    )
    twice = lambda v: np.concatenate([v, v], 1).astype(np.float32)
    weights = weights.reshape(TILE // 2, 2, LANES).swapaxes(0, 1).astype(np.float32)
    return forward, backward, weights, twice(middle), low


def turns(u):
    return (u + MAGIC) - MAGIC


def lanes(shape):
    return lax.broadcasted_iota(jnp.int32, shape, 1)


def rows_of(shape):
    return lax.broadcasted_iota(jnp.int32, shape, 0)


def fetches(x_ref, xv, sems, spans):
    view = xv.reshape(PARTS, ROWS, TILE, LANES)
    groups = []
    for start, size in spans:
        group = []
        for part in range(PARTS):
            copy = pltpu.make_async_copy(
                x_ref.at[:, pl.ds(start, size), pl.ds(part * LANES, LANES)],
                view.at[part, :, pl.ds(start, size), :],
                sems.at[len(groups) * PARTS + part],
            )
            copy.start()
            group.append(copy)
        groups.append(group)
    return groups


def rows_at(xv, a, parts=PARTS):
    where = pl.ds(a, ROWS, stride=TILE)
    return jnp.concatenate([xv[part, where, :] for part in range(parts)], 1)


def counts_kernel(x_ref, edge_ref, step_ref, msg_ref, loc_ref, xv, sems):
    span = TILE // LOADS
    copies = fetches(x_ref, xv, sems, [(t * span, span) for t in range(LOADS)])
    lane128 = lanes((ROWS, 128))
    zero = jnp.zeros((ROWS, WIDTH), jnp.float32)
    half = jnp.zeros((ROWS, TILE), jnp.float32)
    acc_b, acc_a, acc_aw, acc_z = zero, half, half, zero
    acc_s, acc_e = half, half
    prev = None
    for t in range(LOADS):
        for copy in copies[t]:
            copy.wait()
        if prev is None:
            prev = rows_at(xv, 0, 2) * PER_TURN

        def body(i, carry, t=t):
            acc_b, acc_a, acc_aw, acc_z, acc_s, acc_e, prev, first, last = carry
            a = t * span + i
            z = rows_at(xv, a)
            u = z * PER_TURN
            kb = turns(pltpu.roll(u, WIDTH - 1, axis=1) - u)
            ka = turns(u[:, :TILE] - prev)
            here = lane128 == (a % 128)
            first = jnp.where(here, z[:, 0:1], first)
            last = jnp.where(here, z[:, WIDTH - 1 :], last)
            weight = jnp.asarray(TILE - a, jnp.float32)
            above = jnp.maximum(a - 1, 0)
            left = z[:, :TILE]
            acc_s = acc_s + (step_ref[a] * left + step_ref[2 * TILE + above] * ka)
            acc_e = acc_e + (step_ref[TILE + a] * left + step_ref[3 * TILE + above] * ka)
            return (
                acc_b + kb,
                acc_a + ka,
                acc_aw + weight * ka,
                acc_z + z,
                acc_s,
                acc_e,
                u[:, :TILE],
                first,
                last,
            )

        if t % (LOADS // 2) == 0:
            first = jnp.zeros((ROWS, 128), jnp.float32)
            last = jnp.zeros((ROWS, 128), jnp.float32)
        acc_b, acc_a, acc_aw, acc_z, acc_s, acc_e, prev, first, last = lax.fori_loop(
            0,
            span,
            body,
            (acc_b, acc_a, acc_aw, acc_z, acc_s, acc_e, prev, first, last),
            unroll=8,
        )
        if t % (LOADS // 2) == LOADS // 2 - 1:
            part = t // (LOADS // 2)
            msg_ref[pl.ds(8 * part, 8), :] = first
            msg_ref[pl.ds(16 + 8 * part, 8), :] = last
    z_top = rows_at(xv, 0, 2)
    z_bottom = rows_at(xv, TILE - 1, 2)
    below = pltpu.roll(z_top, ROWS - 1, axis=0)
    seam = turns((below - z_bottom) * PER_TURN)
    seam = jnp.where(rows_of((ROWS, TILE)) == ROWS - 1, 0.0, seam)
    acc_a = acc_a + seam
    lane = lanes((ROWS, WIDTH))
    acc_b = jnp.where(lane == WIDTH - 1, 0.0, acc_b)
    falling = (TILE - 1 - lanes((ROWS, TILE))).astype(jnp.float32) * (1.0 / TILE**2)
    total = lambda v: jnp.sum(v, axis=1, keepdims=True)
    edge = lambda k: edge_ref[k : k + 1, :]
    totals, means = [], []
    for c in range(COLS):
        k, z = (v[:, c * TILE : (c + 1) * TILE] for v in (acc_b, acc_z))
        begin = total(z * edge(0) + k * edge(2))
        end = total(z * edge(1) + k * edge(3))
        totals.append(total(k) * (1.0 / TILE) - (end - begin) * PER_TURN)
        means.append(total(k * falling) + begin * PER_TURN)
    first_total, whole_total = totals[0], totals[0] + totals[1]
    begin, end = total(acc_s), total(acc_e)
    down_total = total(acc_a) * (1.0 / TILE) - (end - begin) * PER_TURN
    down_mean = total(acc_aw) * (1.0 / TILE**2) + begin * PER_TURN
    phase_mean = total(acc_z[:, :TILE]) * (1.0 / TILE**2)
    row = rows_of((ROWS, 128))
    edge = jnp.where(row == 0, z_top[0:1, :128], 0.0)
    edge = jnp.where(row == 1, z_top[0:1, 128:], edge)
    edge = jnp.where(row == 2, z_bottom[ROWS - 1 :, :128], edge)
    edge = jnp.where(row == 3, z_bottom[ROWS - 1 :, 128:], edge)
    msg_ref[pl.ds(32, 8), :] = edge
    values = [whole_total, means[0], down_total, down_mean, phase_mean]
    packed = jnp.zeros((ROWS, 128), jnp.float32)
    for index, value in enumerate(values):
        packed = jnp.where(lane128 == index, value, packed)
    msg_ref[pl.ds(40, 8), :] = packed
    packed = jnp.zeros((ROWS, 128), jnp.float32)
    for index, value in enumerate([first_total, means[0], means[1]]):
        packed = jnp.where(lane128 == index, value, packed)
    loc_ref[...] = packed


def across_kernel(got_ref, loc_ref, down_ref, part_ref):
    me = lax.axis_index("col")
    peers = got_ref.shape[0]
    before = jnp.zeros((ROWS, 1), jnp.float32)
    for peer in range(peers - 1):
        border = jnp.zeros((ROWS, 128), jnp.float32)
        for part in range(2):
            right = got_ref[peer + 1, pl.ds(8 * part, 8), :]
            left = got_ref[peer, pl.ds(16 + 8 * part, 8), :]
            border = border + turns((right - left) * PER_TURN)
        crossed = jnp.sum(border, axis=1, keepdims=True) * (1.0 / TILE)
        both = got_ref[peer, pl.ds(40, 8), 0:1] + crossed
        before = before + jnp.where(peer < me, both, 0.0)
    start = got_ref[0, pl.ds(40, 8), :]
    edge = got_ref[0, pl.ds(32, 8), :]
    loc = loc_ref[...]
    lane = lanes((ROWS, 128))
    row = rows_of((ROWS, 128))
    down = start[:, 2:3]
    down_sum = jnp.sum(down, axis=0, keepdims=True)
    info = jnp.where(lane == 0, down_sum, 0.0)
    info = jnp.where(lane == 1, start[0:1, 3:4], info)
    info = jnp.where(lane == 2, start[0:1, 4:5], info)
    down_ref[...] = jnp.where(row == 4, info, edge)
    here = jnp.zeros((ROWS, 1), jnp.float32)
    for index in range(ROWS - 1):
        here = here + jnp.where(rows_of((ROWS, 1)) > index, down[index : index + 1, :], 0.0)
    shared = before + here - start[:, 1:2] + start[:, 3:4]
    one = shared + loc[:, 1:2]
    two = shared + loc[:, 0:1] + loc[:, 2:3]
    part_ref[...] = jnp.where(lane == 0, one, jnp.where(lane == 1, two, 0.0))


def solve_kernel(
    x_ref, fwd_ref, bwd_ref, w_ref, mid_ref, lift_ref, basis_ref, wave_ref, p_ref, sum_ref, xv, yb, sems
):
    spans = []
    for t in range(STEPS):
        spans += [(CHUNK * t, CHUNK), (TILE - CHUNK * (t + 1), CHUNK)]
    for group in fetches(x_ref, xv, sems, spans):
        for copy in group:
            copy.wait()
    lane = lanes((ROWS, WIDTH))
    closed = (lane == TILE - 1) | (lane == WIDTH - 1)

    def loaded(a):
        return rows_at(xv, a) * PER_TURN

    def sources(start):
        u = loaded(jnp.maximum(start - 1, 0))
        here = loaded(start)
        above = turns(here - u)
        out, own = [], []
        for i in range(CHUNK):
            own.append(here)
            after = loaded(jnp.minimum(start + i + 1, TILE - 1))
            below = turns(after - here)
            kb = jnp.where(closed, 0.0, turns(pltpu.roll(here, WIDTH - 1, axis=1) - here))
            out.append((below - above) + (kb - pltpu.roll(kb, 1, axis=1)))
            here, above = after, below
        return [jnp.concatenate(v, 0).astype(jnp.bfloat16) for v in (out, own)]

    def wave(p, a):
        return wave_ref[p * (TILE // 2) + a]

    def gather_low(low, a, top, bottom):
        even, odd = top + bottom, top - bottom
        return (
            low[0] + even,
            low[1] + wave(1, a) * odd,
            low[2] + wave(2, a) * even,
            low[3] + wave(3, a) * odd,
        )

    def transform(t, low):
        top, own_top = sources(t * CHUNK)
        bottom, own_bottom = sources(TILE - CHUNK * (t + 1))
        stack = lambda u, v: jnp.concatenate([u[:, :TILE], u[:, TILE:], v[:, :TILE], v[:, TILE:]], 0)
        left = stack(own_top, own_bottom)
        own = jnp.dot(left, basis_ref[...], preferred_element_type=jnp.float32)
        piece = lambda k, i: own[(k * CHUNK + i) * ROWS : (k * CHUNK + i + 1) * ROWS]
        for i in range(CHUNK):
            pair = [
                jnp.concatenate([piece(2 * side, j), piece(2 * side + 1, j)], 1)
                for side, j in ((0, i), (1, CHUNK - 1 - i))
            ]
            low = gather_low(low, t * CHUNK + i, *pair)
        left = stack(top, bottom)
        left = jnp.concatenate([left, left, left], 1)
        y = jnp.dot(left, fwd_ref[...], preferred_element_type=jnp.float32)
        size = CHUNK * ROWS
        for side in range(2):
            start = (t * CHUNK if side == 0 else TILE - CHUNK * (t + 1)) * ROWS
            start = pl.multiple_of(start, size)
            for c in range(COLS):
                piece = y[(2 * side + c) * size : (2 * side + c + 1) * size]
                yb[pl.ds(start, size), c * TILE : (c + 1) * TILE] = piece
        return low

    def narrow(v):
        return jnp.concatenate([v[:, c * TILE : c * TILE + LANES] for c in range(COLS)], 1)

    def at(a):
        return pl.ds(pl.multiple_of(a * ROWS, ROWS), ROWS)

    def weight(a):
        pair = [jnp.broadcast_to(w_ref[part, pl.ds(a, 1), :], (ROWS, LANES)) for part in range(2)]
        return jnp.concatenate(pair * COLS, 1)

    def eliminate(t, carry):
        top, bottom, low = carry
        for i in range(CHUNK):
            a = t * CHUNK + i
            scale = weight(jnp.maximum(a - 1, 0))
            own_top, own_bottom = yb[at(a), :], yb[at(TILE - 1 - a), :]
            low = gather_low(low, a, narrow(own_top), narrow(own_bottom))
            top = own_top + scale * top
            bottom = own_bottom + scale * bottom
            yb[at(a), :] = top
            yb[at(TILE - 1 - a), :] = bottom
        return top, bottom, low

    zero = jnp.zeros((ROWS, WIDTH), jnp.float32)
    none = (jnp.zeros((ROWS, COLS * LANES), jnp.float32),) * LOW
    low_z = transform(0, none)

    def forward(t, carry):
        carry, low_z = carry
        carry = eliminate(t - 1, carry)
        return carry, transform(t, low_z)

    carry, low_z = lax.fori_loop(1, STEPS, forward, ((zero, zero, none), low_z))
    top, bottom, low_y = eliminate(STEPS - 1, carry)
    lift = []
    for p in range(LOW):
        rows = [
            jnp.concatenate([lift_ref[k : k + 1, :]] * COLS, 1) for k in (p, LOW + p)
        ]
        lift.append(rows[0] * low_z[p] + rows[1] * low_y[p])
    lift[0] = lift[0] * (1.0 / TILE)
    even = mid_ref[0:1, :] * (top + bottom)
    odd = mid_ref[1:2, :] * (top - bottom)
    mid_top, mid_bottom = even + odd, even - odd

    def substitute(t, carry):
        top, bottom, total = carry
        for i in range(CHUNK):
            a = t * CHUNK + (CHUNK - 1 - i)
            scale = weight(a)
            top = scale * (yb[at(a), :] + top)
            bottom = scale * (yb[at(TILE - 1 - a), :] + bottom)
            even = lift[0] + wave(2, a) * lift[2]
            odd = wave(1, a) * lift[1] + wave(3, a) * lift[3]
            for low, value, row in ((even + odd, top, a), (even - odd, bottom, TILE - 1 - a)):
                for part in range(PARTS):
                    piece = value[:, part * LANES : (part + 1) * LANES]
                    if part % 2 == 0:
                        piece = piece + low[:, part // 2 * LANES : (part // 2 + 1) * LANES]
                    yb[at(row), part * LANES : (part + 1) * LANES] = piece
            total = total + narrow(top + bottom)
        return top, bottom, total

    def restore(t):
        size = CHUNK * ROWS
        pieces, starts = [], []
        for side in range(2):
            first = t * CHUNK if side == 0 else TILE - CHUNK * (t + 1)
            starts.append(first)
            block = yb[pl.ds(pl.multiple_of(first * ROWS, size), size), :]
            for c in range(COLS):
                pieces.append(block[:, c * TILE : (c + 1) * TILE])
        value = jnp.concatenate(pieces, 0)
        high = value.astype(jnp.bfloat16)
        low = (value - high.astype(jnp.float32)).astype(jnp.bfloat16)
        left = jnp.concatenate([high, low, high], 1)
        y = jnp.dot(left, bwd_ref[...], preferred_element_type=jnp.float32)
        for side in range(2):
            for i in range(CHUNK):
                where = pl.ds(starts[side] + i, ROWS, stride=TILE)
                for part in range(PARTS):
                    from_row = (2 * side + part // 2) * size + i * ROWS
                    from_lane = (part % 2) * LANES
                    piece = y[from_row : from_row + ROWS, from_lane : from_lane + LANES]
                    p_ref[part, where, :] = xv[part, where, :] + piece

    carry = substitute(STEPS - 1, (mid_bottom, mid_top, none[0]))

    def backward(i, carry):
        t = STEPS - 2 - i
        carry = substitute(t, carry)
        restore(t + 1)
        return carry

    _, _, total = lax.fori_loop(0, STEPS - 1, backward, carry)
    restore(0)
    sum_ref[...] = total


def finish_kernel(p_ref, sum_ref, part_ref, down_ref, out_ref, stage, sems):
    me = lax.axis_index("row")
    peers = down_ref.shape[0]
    before = jnp.zeros((1, 1), jnp.float32)
    for peer in range(peers - 1):
        border = turns((down_ref[peer + 1, 0:2, :] - down_ref[peer, 2:4, :]) * PER_TURN)
        border = jnp.sum(jnp.sum(border, axis=1, keepdims=True), axis=0, keepdims=True)
        both = border * (1.0 / TILE) + down_ref[peer, 4:5, 0:1]
        before = before + jnp.where(peer < me, both, 0.0)
    shared = before - down_ref[0, 4:5, 1:2]
    mean = down_ref[0, 4:5, 2:3]
    shift = []
    for c in range(COLS):
        level = sum_ref[:, c * LANES : c * LANES + 1] * (1.0 / (16.0 * TILE))
        value = -mean - TURN * (part_ref[:, c : c + 1] + shared + level)
        shift.append(jnp.broadcast_to(value, (ROWS, LANES)))
    copies = []
    for row in range(ROWS):
        rows = pl.ds(row * TILE, TILE)
        for part in range(PARTS):
            cols = slice(part * LANES, (part + 1) * LANES)
            stage[rows, cols] = p_ref[part, rows, :] + shift[part // 2][row : row + 1, :]
        copy = pltpu.make_async_copy(stage.at[rows, :], out_ref.at[rows, :], sems.at[row])
        copy.start()
        copies.append(copy)
    for copy in copies:
        copy.wait()


VMEM = pl.BlockSpec(memory_space=pltpu.VMEM)
HBM = pl.BlockSpec(memory_space=pltpu.HBM)
SMEM = pl.BlockSpec(memory_space=pltpu.SMEM)


def f32(*shape):
    return jax.ShapeDtypeStruct(shape, jnp.float32)


def to_all(x, axis):
    peers = lax.axis_size(axis)
    return lax.all_to_all(jnp.broadcast_to(x[None], (peers, *x.shape)), axis, 0, 0, tiled=True)


def per_device(phase):
    *big, low = tables()
    forward, backward, weights, middle = (jnp.asarray(t) for t in big)
    low = {k: jnp.asarray(v) for k, v in low.items()}
    grid = pltpu.with_memory_space_constraint(phase.reshape(ROWS, TILE, WIDTH), pltpu.HBM)
    msg, loc = pl.pallas_call(
        counts_kernel,
        out_shape=(f32(MSG, 128), f32(ROWS, 128)),
        in_specs=[HBM, VMEM, SMEM],
        out_specs=(VMEM, VMEM),
        scratch_shapes=[
            pltpu.VMEM((PARTS, ROWS * TILE, LANES), jnp.float32),
            pltpu.SemaphoreType.DMA((LOADS * PARTS,)),
        ],
        compiler_params=pltpu.CompilerParams(vmem_limit_bytes=8 << 20),
        cost_estimate=pl.CostEstimate(flops=1 << 24, bytes_accessed=4 << 20, transcendentals=0),
        name="counts",
    )(grid, low["edges"], low["steps"])
    got = to_all(msg, "col")
    down, part = pl.pallas_call(
        across_kernel,
        out_shape=(f32(ROWS, 128), f32(ROWS, 128)),
        in_specs=[VMEM, VMEM],
        out_specs=(VMEM, VMEM),
        name="across",
    )(got, loc)
    downs = to_all(down, "row")
    p, total = pl.pallas_call(
        solve_kernel,
        out_shape=(f32(PARTS, ROWS * TILE, LANES), f32(ROWS, COLS * LANES)),
        in_specs=[HBM, VMEM, VMEM, VMEM, VMEM, VMEM, VMEM, SMEM],
        out_specs=(VMEM, VMEM),
        scratch_shapes=[
            pltpu.VMEM((PARTS, ROWS * TILE, LANES), jnp.float32),
            pltpu.VMEM((ROWS * TILE, WIDTH), jnp.float32),
            pltpu.SemaphoreType.DMA((2 * STEPS * PARTS,)),
        ],
        compiler_params=pltpu.CompilerParams(vmem_limit_bytes=14 << 20),
        cost_estimate=pl.CostEstimate(flops=4 << 30, bytes_accessed=8 << 20, transcendentals=0),
        name="solve",
    )(grid, forward, backward, weights, middle, low["lift"], low["basis"], low["waves"])
    return pl.pallas_call(
        finish_kernel,
        out_shape=f32(ROWS * TILE, WIDTH),
        in_specs=[VMEM, VMEM, VMEM, VMEM],
        out_specs=HBM,
        scratch_shapes=[
            pltpu.VMEM((ROWS * TILE, WIDTH), jnp.float32),
            pltpu.SemaphoreType.DMA((ROWS,)),
        ],
        compiler_params=pltpu.CompilerParams(vmem_limit_bytes=8 << 20),
        name="finish",
    )(pltpu.with_memory_space_constraint(p, pltpu.VMEM), total, part, downs)


def solution(mesh):
    return jax.shard_map(
        per_device, mesh=mesh, in_specs=(P("row", "col"),), out_specs=P("row", "col"), check_vma=False
    )
```

```python
import math

import jax
import jax.numpy as jnp
import ml_dtypes
import numpy as np
from jax import lax
from jax.experimental import pallas as pl
from jax.experimental.pallas import tpu as pltpu
from jax.sharding import PartitionSpec as P

TILE = 256
TURN = 2.0 * math.pi
PER_TURN = 1.0 / TURN
MAGIC = 1.5 * 2.0**23
ROWS = 8
COLS = 2
WIDTH = COLS * TILE
LANES = 128
PARTS = WIDTH // LANES
PITCH = TILE + 8
LOADS = 8
CHUNK = 16
STEPS = TILE // (2 * CHUNK)
MSG = 48
LOW = 4


def split_terms(table, terms):
    parts, rest = [], np.asarray(table, np.float64)
    for _ in range(terms):
        part = rest.astype(ml_dtypes.bfloat16)
        parts.append(part)
        rest = rest - part.astype(np.float64)
    return parts


def tables():
    q = np.arange(TILE, dtype=np.float64)
    c = np.cos(math.pi * q[:, None] * (2.0 * q[None, :] + 1.0) / (2.0 * TILE))
    c *= math.sqrt(2.0 / TILE)
    c[0] *= math.sqrt(0.5)
    step = np.zeros_like(c.T)
    step[:-1] = c.T[:-1] - c.T[1:]
    forward = np.concatenate(split_terms(c.T, 2) + split_terms(step, 2), 0)
    across = np.zeros((TILE, TILE))
    index = np.arange(TILE - 1)
    across[index + 1, index], across[index, index] = 1.0, -1.0
    high, low = split_terms(TURN * c, 2)
    backward = np.concatenate([high, high, low], 0)
    mu = 4.0 * np.sin(math.pi * q / (2.0 * TILE)) ** 2
    pivot = [1.0 + mu]
    for _ in range(TILE // 2 - 1):
        pivot.append(2.0 + mu - 1.0 / pivot[-1])
    weights = np.stack([1.0 / d for d in pivot])
    last = pivot[-1]
    even = np.zeros_like(mu)
    even[1:] = 0.5 / (last[1:] - 1.0)
    odd = 0.5 / (last + 1.0)
    middle = np.stack([even, odd])
    freq = np.arange(LOW, dtype=np.float32)
    wave = np.float32(2.0) * np.cos(np.float32(math.pi) * freq / np.float32(TILE))
    held = (wave[:, None] + wave[None, :]).astype(np.float32) - np.float32(4.0)
    exact = mu[:LOW, None] + mu[None, :LOW]
    delta = np.zeros((LOW, LOW))
    known = exact > 0.0
    delta[known] = exact[known] / -held[known].astype(np.float64) - 1.0
    lift = np.zeros((2 * LOW, LANES))
    lift[:LOW, :LOW] = delta
    lift[LOW:, :LOW][known] = delta[known] / exact[known]
    basis = np.zeros((TILE, LANES))
    basis[:, :LOW] = c[:LOW].T
    starts = (delta[0, :LOW] * c[:LOW, 0]) @ c[:LOW]
    ends = (delta[0, :LOW] * c[:LOW, -1]) @ c[:LOW]
    after = lambda g: np.cumsum(g[::-1])[::-1] - g
    edges = np.zeros((8, TILE))
    edges[:4] = np.stack([starts, ends, -TURN * after(starts), -TURN * after(ends)]) / TILE
    low = dict(
        lift=lift.astype(np.float32),
        basis=np.concatenate([across, basis], 1).astype(ml_dtypes.bfloat16),
        across=across.astype(ml_dtypes.bfloat16),
        waves=c[:LOW, : TILE // 2].astype(np.float32).reshape(-1),
        edges=edges.astype(np.float32),
        steps=edges[:4].astype(np.float32).reshape(-1),
    )
    twice = lambda v: np.concatenate([v, v], 1).astype(np.float32)
    weights = weights.reshape(TILE // 2, 2, LANES).swapaxes(0, 1).astype(np.float32)
    return forward, backward, weights, twice(middle), low


def turns(u):
    return (u + MAGIC) - MAGIC


def lanes(shape):
    return lax.broadcasted_iota(jnp.int32, shape, 1)


def rows_of(shape):
    return lax.broadcasted_iota(jnp.int32, shape, 0)


def span_copies(x_ref, xv, sems, start, size, t):
    view = xv.reshape(PARTS, ROWS, PITCH, LANES)
    copies = []
    for part in range(PARTS):
        ends = (
            x_ref.at[:, pl.ds(start, size), pl.ds(part * LANES, LANES)],
            view.at[part, :, pl.ds(start, size), :],
        )
        copies.append(pltpu.make_async_copy(*ends, sems.at[t * PARTS + part]))
    return copies


def side_start(t, side):
    start = CHUNK * t if side == 0 else TILE - CHUNK * (t + 1)
    return start if isinstance(start, int) else pl.multiple_of(start, CHUNK)


def field_copies(x_ref, xv, sems, t, out=False):
    view = xv.reshape(PARTS, ROWS, PITCH, LANES)
    copies = []
    for side in range(2):
        for part in range(PARTS):
            span = pl.ds(side_start(t, side), CHUNK)
            ends = (x_ref.at[:, span, pl.ds(part * LANES, LANES)], view.at[part, :, span, :])
            sem = sems.at[(2 * t + side) * PARTS + part]
            copies.append(pltpu.make_async_copy(*(ends[::-1] if out else ends), sem))
    return copies


def row_copies(y_ref, yb, sems, t, out=False):
    copies = []
    for side in range(2):
        span = pl.ds(side_start(t, side) * ROWS, CHUNK * ROWS)
        ends = (y_ref.at[span, :], yb.at[span, :])
        copies.append(pltpu.make_async_copy(*(ends[::-1] if out else ends), sems.at[2 * t + side]))
    return copies


def start_all(copies):
    for copy in copies:
        copy.start()


def wait_all(copies):
    for copy in copies:
        copy.wait()


def rows_at(xv, a, parts=PARTS):
    where = pl.ds(a, ROWS, stride=PITCH)
    return jnp.concatenate([xv[part, where, :] for part in range(parts)], 1)


def counts_kernel(
    x_ref, edge_hbm, step_hbm, across_hbm, all_ref, loc_ref,
    msg_ref, xv, edge_ref, step_ref, across_ref, sems, table_sems
):
    tables_in = [
        pltpu.make_async_copy(step_hbm, step_ref, table_sems.at[0]),
        pltpu.make_async_copy(edge_hbm, edge_ref, table_sems.at[1]),
        pltpu.make_async_copy(across_hbm, across_ref, table_sems.at[2]),
    ]
    for copy in tables_in:
        copy.start()
    span = TILE // LOADS
    for t in range(LOADS):
        start_all(span_copies(x_ref, xv, sems, t * span, span, t))
    for copy in tables_in:
        copy.wait()
    lane128 = lanes((ROWS, 128))
    zero = jnp.zeros((ROWS, WIDTH), jnp.float32)
    half = jnp.zeros((ROWS, TILE), jnp.float32)
    acc_b, acc_a, acc_aw, acc_z = zero, half, half, zero
    acc_s, acc_e = half, half
    msg_ref[...] = jnp.zeros((MSG, LANES), jnp.float32)

    def chunk(t, carry):
        acc_b, acc_m, acc_a, acc_aw, acc_z, acc_s, acc_e, prev = carry

        wait_all(span_copies(x_ref, xv, sems, pl.multiple_of(t * span, span), span, t))
        half = t // (LOADS // 2)
        near = pl.ds(pl.multiple_of(8 * half, 8), 8)
        far = pl.ds(pl.multiple_of(16 + 8 * half, 8), 8)
        first, last = msg_ref[near, :], msg_ref[far, :]
        own = []
        for i in range(span):
            a = t * span + i
            z = rows_at(xv, a)
            u = z * PER_TURN
            own.append(u)
            if i == 0:
                prev = jnp.where(t == 0, u[:, :TILE], prev)
            ka = turns(u[:, :TILE] - prev)
            edge = pltpu.roll(u[:, TILE - LANES : TILE], 1, axis=1)
            acc_m = acc_m + turns(u[:, TILE : TILE + LANES] - edge)
            here = lane128 == (a % LANES)
            first = jnp.where(here, z[:, 0:1], first)
            last = jnp.where(here, z[:, WIDTH - 1 :], last)
            weight = (TILE - a).astype(jnp.float32)
            above = jnp.maximum(a - 1, 0)
            left = z[:, :TILE]
            acc_s = acc_s + (step_ref[a] * left + step_ref[2 * TILE + above] * ka)
            acc_e = acc_e + (step_ref[TILE + a] * left + step_ref[3 * TILE + above] * ka)
            acc_a = acc_a + ka
            acc_aw = acc_aw + weight * ka
            acc_z = acc_z + z
            prev = u[:, :TILE]
        msg_ref[near, :] = first
        msg_ref[far, :] = last
        own = jnp.concatenate(own, 0).astype(jnp.bfloat16)
        own = jnp.concatenate([own[:, :TILE], own[:, TILE:]], 0)
        kb = turns(jnp.dot(own, across_ref[...], preferred_element_type=jnp.float32))
        for i in range(span):
            pair = [kb[(c * span + i) * ROWS : (c * span + i + 1) * ROWS] for c in range(COLS)]
            acc_b = acc_b + jnp.concatenate(pair, 1)
        return acc_b, acc_m, acc_a, acc_aw, acc_z, acc_s, acc_e, prev

    start = (acc_b, jnp.zeros((ROWS, LANES), jnp.float32), acc_a, acc_aw, acc_z, acc_s, acc_e, half)
    acc_b, acc_m, acc_a, acc_aw, acc_z, acc_s, acc_e, _ = lax.fori_loop(0, LOADS, chunk, start
    )
    z_top = rows_at(xv, 0, 2)
    z_bottom = rows_at(xv, TILE - 1, 2)
    below = pltpu.roll(z_top, ROWS - 1, axis=0)
    seam = turns((below - z_bottom) * PER_TURN)
    seam = jnp.where(rows_of((ROWS, TILE)) == ROWS - 1, 0.0, seam)
    acc_a = acc_a + seam
    falling = (TILE - 1 - lanes((ROWS, TILE))).astype(jnp.float32) * (1.0 / TILE**2)
    total = lambda v: jnp.sum(v, axis=1, keepdims=True)
    edge = lambda k: edge_ref[k : k + 1, :]
    totals, means = [], []
    for c in range(COLS):
        k, z = (v[:, c * TILE : (c + 1) * TILE] for v in (acc_b, acc_z))
        begin = total(z * edge(0) + k * edge(2))
        end = total(z * edge(1) + k * edge(3))
        totals.append(total(k) * (1.0 / TILE) - (end - begin) * PER_TURN)
        means.append(total(k * falling) + begin * PER_TURN)
    totals[0] = totals[0] + acc_m[:, 0:1] * (1.0 / TILE)
    first_total, whole_total = totals[0], totals[0] + totals[1]
    begin, end = total(acc_s), total(acc_e)
    down_total = total(acc_a) * (1.0 / TILE) - (end - begin) * PER_TURN
    down_mean = total(acc_aw) * (1.0 / TILE**2) + begin * PER_TURN
    phase_mean = total(acc_z[:, :TILE]) * (1.0 / TILE**2)
    row = rows_of((ROWS, 128))
    edge = jnp.where(row == 0, z_top[0:1, :128], 0.0)
    edge = jnp.where(row == 1, z_top[0:1, 128:], edge)
    edge = jnp.where(row == 2, z_bottom[ROWS - 1 :, :128], edge)
    edge = jnp.where(row == 3, z_bottom[ROWS - 1 :, 128:], edge)
    msg_ref[pl.ds(32, 8), :] = edge
    values = [whole_total, means[0], down_total, down_mean, phase_mean]
    packed = jnp.zeros((ROWS, 128), jnp.float32)
    for index, value in enumerate(values):
        packed = jnp.where(lane128 == index, value, packed)
    msg_ref[pl.ds(40, 8), :] = packed
    packed = jnp.zeros((ROWS, 128), jnp.float32)
    for index, value in enumerate([first_total, means[0], means[1]]):
        packed = jnp.where(lane128 == index, value, packed)
    loc_ref[...] = packed
    for peer in range(all_ref.shape[0]):
        all_ref[peer] = msg_ref[...]


def across_kernel(got_ref, loc_ref, down_ref, part_ref):
    me = lax.axis_index("col")
    peers = got_ref.shape[0]
    before = jnp.zeros((ROWS, 1), jnp.float32)
    for peer in range(peers - 1):
        border = jnp.zeros((ROWS, 128), jnp.float32)
        for part in range(2):
            right = got_ref[peer + 1, pl.ds(8 * part, 8), :]
            left = got_ref[peer, pl.ds(16 + 8 * part, 8), :]
            border = border + turns((right - left) * PER_TURN)
        crossed = jnp.sum(border, axis=1, keepdims=True) * (1.0 / TILE)
        both = got_ref[peer, pl.ds(40, 8), 0:1] + crossed
        before = before + jnp.where(peer < me, both, 0.0)
    start = got_ref[0, pl.ds(40, 8), :]
    edge = got_ref[0, pl.ds(32, 8), :]
    loc = loc_ref[...]
    lane = lanes((ROWS, 128))
    row = rows_of((ROWS, 128))
    down = start[:, 2:3]
    down_sum = jnp.sum(down, axis=0, keepdims=True)
    info = jnp.where(lane == 0, down_sum, 0.0)
    info = jnp.where(lane == 1, start[0:1, 3:4], info)
    info = jnp.where(lane == 2, start[0:1, 4:5], info)
    info = jnp.where(row == 4, info, edge)
    for peer in range(down_ref.shape[0]):
        down_ref[peer] = info
    here = jnp.zeros((ROWS, 1), jnp.float32)
    for index in range(ROWS - 1):
        here = here + jnp.where(rows_of((ROWS, 1)) > index, down[index : index + 1, :], 0.0)
    shared = before + here - start[:, 1:2] + start[:, 3:4]
    one = shared + loc[:, 1:2]
    two = shared + loc[:, 0:1] + loc[:, 2:3]
    part_ref[...] = jnp.where(lane == 0, one, jnp.where(lane == 1, two, 0.0))


def at(a):
    return pl.ds(pl.multiple_of(a * ROWS, ROWS), ROWS)


def weight(w_ref, a):
    pair = [jnp.broadcast_to(w_ref[part, pl.ds(a, 1), :], (ROWS, LANES)) for part in range(2)]
    return jnp.concatenate(pair * COLS, 1)


def narrow(v):
    return jnp.concatenate([v[:, c * TILE : c * TILE + LANES] for c in range(COLS)], 1)


def forward_kernel(
    x_ref, fwd_ref, w_ref, mid_ref, lift_ref, basis_ref, wave_ref, y_ref, ends_ref,
    xv, yb, in_sems, out_sems
):
    for t in range(STEPS):
        start_all(field_copies(x_ref, xv, in_sems, t))
    def loaded(a):
        return rows_at(xv, a) * PER_TURN

    def sources(start):
        u = loaded(jnp.maximum(start - 1, 0))
        here = loaded(start)
        above = turns(here - u)
        out, own = [], []
        for i in range(CHUNK):
            own.append(here)
            after = loaded(jnp.minimum(start + i + 1, TILE - 1))
            below = turns(after - here)
            out.append(below - above)
            here, above = after, below
        return [jnp.concatenate(v, 0).astype(jnp.bfloat16) for v in (out, own)]

    def wave(p, a):
        return wave_ref[p * (TILE // 2) + a]

    def gather_low(low, a, top, bottom):
        even, odd = top + bottom, top - bottom
        return (
            low[0] + even,
            low[1] + wave(1, a) * odd,
            low[2] + wave(2, a) * even,
            low[3] + wave(3, a) * odd,
        )

    def transform(t, low):
        top, own_top = sources(t * CHUNK)
        bottom, own_bottom = sources(TILE - CHUNK * (t + 1))
        stack = lambda u, v: jnp.concatenate([u[:, :TILE], u[:, TILE:], v[:, :TILE], v[:, TILE:]], 0)
        left = stack(own_top, own_bottom)
        both = jnp.dot(left, basis_ref[...], preferred_element_type=jnp.float32)
        kb, own = turns(both[:, :TILE]).astype(jnp.bfloat16), both[:, TILE:]
        piece = lambda k, i: own[(k * CHUNK + i) * ROWS : (k * CHUNK + i + 1) * ROWS]
        for i in range(CHUNK):
            pair = [
                jnp.concatenate([piece(2 * side, j), piece(2 * side + 1, j)], 1)
                for side, j in ((0, i), (1, CHUNK - 1 - i))
            ]
            low = gather_low(low, t * CHUNK + i, *pair)
        left = stack(top, bottom)
        left = jnp.concatenate([left, left, kb, kb], 1)
        y = jnp.dot(left, fwd_ref[...], preferred_element_type=jnp.float32)
        size = CHUNK * ROWS
        for side in range(2):
            start = (t * CHUNK if side == 0 else TILE - CHUNK * (t + 1)) * ROWS
            start = pl.multiple_of(start, size)
            for c in range(COLS):
                piece = y[(2 * side + c) * size : (2 * side + c + 1) * size]
                yb[pl.ds(start, size), c * TILE : (c + 1) * TILE] = piece
        return low

    def eliminate(t, carry):
        top, bottom, low = carry
        for i in range(CHUNK):
            a = t * CHUNK + i
            scale = weight(w_ref, jnp.maximum(a - 1, 0))
            own_top, own_bottom = yb[at(a), :], yb[at(TILE - 1 - a), :]
            low = gather_low(low, a, narrow(own_top), narrow(own_bottom))
            top = own_top + scale * top
            bottom = own_bottom + scale * bottom
            yb[at(a), :] = top
            yb[at(TILE - 1 - a), :] = bottom
        return top, bottom, low

    zero = jnp.zeros((ROWS, WIDTH), jnp.float32)
    none = (jnp.zeros((ROWS, COLS * LANES), jnp.float32),) * LOW
    for t in range(2):
        wait_all(field_copies(x_ref, xv, in_sems, t))
    low_z = transform(0, none)

    def forward(t, carry):
        carry, low_z = carry

        @pl.when(t + 1 < STEPS)
        def _():
            wait_all(field_copies(x_ref, xv, in_sems, t + 1))

        carry = eliminate(t - 1, carry)
        low_z = transform(t, low_z)
        start_all(row_copies(y_ref, yb, out_sems, t - 1, out=True))
        return carry, low_z

    carry, low_z = lax.fori_loop(1, STEPS, forward, ((zero, zero, none), low_z))
    top, bottom, low_y = eliminate(STEPS - 1, carry)
    start_all(row_copies(y_ref, yb, out_sems, STEPS - 1, out=True))
    lift = []
    for p in range(LOW):
        rows = [
            jnp.concatenate([lift_ref[k : k + 1, :]] * COLS, 1) for k in (p, LOW + p)
        ]
        lift.append(rows[0] * low_z[p] + rows[1] * low_y[p])
    lift[0] = lift[0] * (1.0 / TILE)
    even = mid_ref[0:1, :] * (top + bottom)
    odd = mid_ref[1:2, :] * (top - bottom)
    ends_ref[0:ROWS, :] = even + odd
    ends_ref[ROWS : 2 * ROWS, :] = even - odd
    for p in range(LOW):
        for c in range(COLS):
            ends_ref[(2 + p) * ROWS : (3 + p) * ROWS, c * TILE : c * TILE + LANES] = lift[p][
                :, c * LANES : (c + 1) * LANES
            ]
    for t in range(STEPS):
        wait_all(row_copies(y_ref, yb, out_sems, t, out=True))


def backward_kernel(
    x_ref, y_ref, ends_ref, bwd_ref, w_ref, wave_ref, p_ref, sum_ref,
    xv, yb, xb, x_sems, y_sems, out_sems
):
    for t in reversed(range(STEPS)):
        start_all(row_copies(y_ref, yb, y_sems, t))
        start_all(field_copies(x_ref, xv, x_sems, t))
    def wave(p, a):
        return wave_ref[p * (TILE // 2) + a]

    mid_top, mid_bottom = (ends_ref[k * ROWS : (k + 1) * ROWS, :] for k in range(2))
    lift = [narrow(ends_ref[(2 + p) * ROWS : (3 + p) * ROWS, :]) for p in range(LOW)]

    def substitute(t, carry):
        top, bottom, total = carry
        wait_all(row_copies(y_ref, yb, y_sems, t))
        for i in range(CHUNK):
            a = t * CHUNK + (CHUNK - 1 - i)
            scale = weight(w_ref, a)
            top = scale * (yb[at(a), :] + top)
            bottom = scale * (yb[at(TILE - 1 - a), :] + bottom)
            even = lift[0] + wave(2, a) * lift[2]
            odd = wave(1, a) * lift[1] + wave(3, a) * lift[3]
            for low, value, row in ((even + odd, top, a), (even - odd, bottom, TILE - 1 - a)):
                for part in range(PARTS):
                    piece = value[:, part * LANES : (part + 1) * LANES]
                    if part % 2 == 0:
                        piece = piece + low[:, part // 2 * LANES : (part // 2 + 1) * LANES]
                    xb[at(row), part * LANES : (part + 1) * LANES] = piece
            total = total + narrow(top + bottom)
        return top, bottom, total

    def restore(t):
        wait_all(field_copies(x_ref, xv, x_sems, t))
        size = CHUNK * ROWS
        pieces, starts = [], []
        for side in range(2):
            first = t * CHUNK if side == 0 else TILE - CHUNK * (t + 1)
            starts.append(first)
            block = xb[pl.ds(pl.multiple_of(first * ROWS, size), size), :]
            for c in range(COLS):
                pieces.append(block[:, c * TILE : (c + 1) * TILE])
        value = jnp.concatenate(pieces, 0)
        high = value.astype(jnp.bfloat16)
        low = (value - high.astype(jnp.float32)).astype(jnp.bfloat16)
        left = jnp.concatenate([high, low, high], 1)
        y = jnp.dot(left, bwd_ref[...], preferred_element_type=jnp.float32)
        for side in range(2):
            for i in range(CHUNK):
                where = pl.ds(starts[side] + i, ROWS, stride=PITCH)
                for part in range(PARTS):
                    from_row = (2 * side + part // 2) * size + i * ROWS
                    from_lane = (part % 2) * LANES
                    piece = y[from_row : from_row + ROWS, from_lane : from_lane + LANES]
                    xv[part, where, :] = xv[part, where, :] + piece
        start_all(field_copies(p_ref, xv, out_sems, t, out=True))

    carry = substitute(STEPS - 1, (mid_bottom, mid_top, jnp.zeros((ROWS, COLS * LANES), jnp.float32)))

    def backward(i, carry):
        t = STEPS - 2 - i
        carry = substitute(t, carry)
        restore(t + 1)
        return carry

    _, _, total = lax.fori_loop(0, STEPS - 1, backward, carry)
    restore(0)
    sum_ref[...] = total
    for t in range(STEPS):
        wait_all(field_copies(p_ref, xv, out_sems, t, out=True))


def finish_kernel(p_ref, sum_ref, part_ref, down_ref, out_ref, stage, in_sems, out_sems):
    def block(row, out):
        rows = stage.at[row]
        ends = (rows, out_ref.at[row]) if out else (p_ref.at[row], rows)
        return pltpu.make_async_copy(*ends, (out_sems if out else in_sems).at[row])

    for row in range(ROWS):
        block(row, False).start()
    me = lax.axis_index("row")
    peers = down_ref.shape[0]
    before = jnp.zeros((1, 1), jnp.float32)
    for peer in range(peers - 1):
        border = turns((down_ref[peer + 1, 0:2, :] - down_ref[peer, 2:4, :]) * PER_TURN)
        border = jnp.sum(jnp.sum(border, axis=1, keepdims=True), axis=0, keepdims=True)
        both = border * (1.0 / TILE) + down_ref[peer, 4:5, 0:1]
        before = before + jnp.where(peer < me, both, 0.0)
    shared = before - down_ref[0, 4:5, 1:2]
    mean = down_ref[0, 4:5, 2:3]
    shift = []
    for c in range(COLS):
        level = sum_ref[:, c * LANES : c * LANES + 1] * (1.0 / (16.0 * TILE))
        value = -mean - TURN * (part_ref[:, c : c + 1] + shared + level)
        shift.append(jnp.broadcast_to(value, (ROWS, LANES)))
    shift = jnp.concatenate([shift[part // 2] for part in range(PARTS)], 1)
    for row in range(ROWS):
        block(row, False).wait()
        stage[row] = stage[row] + shift[row : row + 1, :]
        block(row, True).start()
    for row in range(ROWS):
        block(row, True).wait()


VMEM = pl.BlockSpec(memory_space=pltpu.VMEM)
HBM = pl.BlockSpec(memory_space=pltpu.HBM)
FIELD = pltpu.VMEM((PARTS, ROWS * PITCH, LANES), jnp.float32)
SMEM = pl.BlockSpec(memory_space=pltpu.SMEM)


def f32(*shape):
    return jax.ShapeDtypeStruct(shape, jnp.float32)


def in_hbm(x):
    return pltpu.with_memory_space_constraint(x, pltpu.HBM)


def to_all(x, axis):
    return lax.all_to_all(x, axis, 0, 0, tiled=True)


def per_device(phase):
    *big, low = tables()
    forward, backward, weights, middle = (jnp.asarray(t) for t in big)
    low = {k: jnp.asarray(v) for k, v in low.items()}
    grid = in_hbm(phase.reshape(ROWS, TILE, WIDTH))
    peers = {axis: lax.axis_size(axis) for axis in ("row", "col")}
    msg, loc = pl.pallas_call(
        counts_kernel,
        out_shape=(
            f32(peers["col"], MSG, LANES),
            f32(ROWS, LANES),
        ),
        in_specs=[HBM] * 4,
        out_specs=(VMEM,) * 2,
        scratch_shapes=[
            pltpu.VMEM((MSG, LANES), jnp.float32),
            FIELD,
            pltpu.VMEM((8, TILE), jnp.float32),
            pltpu.SMEM((4 * TILE,), jnp.float32),
            pltpu.VMEM((TILE, TILE), jnp.bfloat16),
            pltpu.SemaphoreType.DMA((LOADS * PARTS,)),
            pltpu.SemaphoreType.DMA((3,)),
        ],
        compiler_params=pltpu.CompilerParams(vmem_limit_bytes=8 << 20),
        cost_estimate=pl.CostEstimate(flops=1 << 30, bytes_accessed=4 << 20, transcendentals=0),
        name="counts",
    )(grid, in_hbm(low["edges"]), in_hbm(low["steps"]), in_hbm(low["across"]))
    got = to_all(msg, "col")
    yb, ends = pl.pallas_call(
        forward_kernel,
        out_shape=(pltpu.HBM((ROWS * TILE, WIDTH), jnp.float32), f32((2 + LOW) * ROWS, WIDTH)),
        in_specs=[HBM] + [VMEM] * 5 + [SMEM],
        out_specs=(HBM, VMEM),
        scratch_shapes=[
            pltpu.VMEM((PARTS, ROWS * PITCH, LANES), jnp.float32),
            pltpu.VMEM((ROWS * TILE, WIDTH), jnp.float32),
            pltpu.SemaphoreType.DMA((2 * STEPS * PARTS,)),
            pltpu.SemaphoreType.DMA((2 * STEPS,)),
        ],
        compiler_params=pltpu.CompilerParams(vmem_limit_bytes=12 << 20),
        cost_estimate=pl.CostEstimate(flops=8 << 30, bytes_accessed=8 << 20, transcendentals=0),
        name="ahead",
    )(grid, forward, weights, middle, low["lift"], low["basis"], low["waves"])
    down, part = pl.pallas_call(
        across_kernel,
        out_shape=(f32(peers["row"], ROWS, LANES), f32(ROWS, LANES)),
        in_specs=[VMEM, VMEM],
        out_specs=(VMEM, VMEM),
        compiler_params=pltpu.CompilerParams(vmem_limit_bytes=4 << 20),
        name="across",
    )(got, loc)
    downs = to_all(down, "row")
    p, total = pl.pallas_call(
        backward_kernel,
        out_shape=(pltpu.HBM((ROWS, TILE, WIDTH), jnp.float32), f32(ROWS, COLS * LANES)),
        in_specs=[HBM, HBM] + [VMEM] * 3 + [SMEM],
        out_specs=(HBM, VMEM),
        scratch_shapes=[
            pltpu.VMEM((PARTS, ROWS * PITCH, LANES), jnp.float32),
            pltpu.VMEM((ROWS * TILE, WIDTH), jnp.float32),
            pltpu.VMEM((ROWS * TILE, WIDTH), jnp.float32),
            pltpu.SemaphoreType.DMA((2 * STEPS * PARTS,)),
            pltpu.SemaphoreType.DMA((2 * STEPS,)),
            pltpu.SemaphoreType.DMA((2 * STEPS * PARTS,)),
        ],
        compiler_params=pltpu.CompilerParams(vmem_limit_bytes=16 << 20),
        cost_estimate=pl.CostEstimate(flops=8 << 30, bytes_accessed=8 << 20, transcendentals=0),
        name="back",
    )(grid, in_hbm(yb), ends, backward, weights, low["waves"])
    out = pl.pallas_call(
        finish_kernel,
        out_shape=f32(ROWS, TILE, WIDTH),
        in_specs=[HBM, VMEM, VMEM, VMEM],
        out_specs=HBM,
        scratch_shapes=[
            pltpu.VMEM((ROWS, TILE, WIDTH), jnp.float32),
            pltpu.SemaphoreType.DMA((ROWS,)),
            pltpu.SemaphoreType.DMA((ROWS,)),
        ],
        compiler_params=pltpu.CompilerParams(vmem_limit_bytes=8 << 20),
        name="finish",
    )(in_hbm(p), total, part, downs)
    return out.reshape(phase.shape)


def solution(mesh):
    return jax.shard_map(
        per_device, mesh=mesh, in_specs=(P("row", "col"),), out_specs=P("row", "col"), check_vma=False
    )
```

```python
import math

import jax
import jax.numpy as jnp
import ml_dtypes
import numpy as np
from jax import lax
from jax.experimental import pallas as pl
from jax.experimental.pallas import tpu as pltpu
from jax.sharding import PartitionSpec as P

TILE = 256
TURN = 2.0 * math.pi
PER_TURN = 1.0 / TURN
MAGIC = 1.5 * 2.0**23
ROWS = 8
COLS = 2
WIDTH = COLS * TILE
LANES = 128
PARTS = WIDTH // LANES
PITCH = TILE + 8
SUB = 8
BLOCKS = TILE // SUB * PARTS
BLOCK_PITCH = BLOCKS + 1
LOADS = 8
CHUNK = 16
STEPS = TILE // (2 * CHUNK)
MSG = 48
LOW = 4


def split_terms(table, terms):
    parts, rest = [], np.asarray(table, np.float64)
    for _ in range(terms):
        part = rest.astype(ml_dtypes.bfloat16)
        parts.append(part)
        rest = rest - part.astype(np.float64)
    return parts


def tables():
    q = np.arange(TILE, dtype=np.float64)
    c = np.cos(math.pi * q[:, None] * (2.0 * q[None, :] + 1.0) / (2.0 * TILE))
    c *= math.sqrt(2.0 / TILE)
    c[0] *= math.sqrt(0.5)
    step = np.zeros_like(c.T)
    step[:-1] = c.T[:-1] - c.T[1:]
    forward = np.concatenate(split_terms(c.T, 2) + split_terms(step, 2), 0)
    across = np.zeros((TILE, TILE))
    index = np.arange(TILE - 1)
    across[index + 1, index], across[index, index] = 1.0, -1.0
    high, low = split_terms(TURN * c, 2)
    backward = np.concatenate([high, high, low], 0)
    mu = 4.0 * np.sin(math.pi * q / (2.0 * TILE)) ** 2
    pivot = [1.0 + mu]
    for _ in range(TILE // 2 - 1):
        pivot.append(2.0 + mu - 1.0 / pivot[-1])
    weights = np.stack([1.0 / d for d in pivot])
    last = pivot[-1]
    even = np.zeros_like(mu)
    even[1:] = 0.5 / (last[1:] - 1.0)
    odd = 0.5 / (last + 1.0)
    middle = np.stack([even, odd])
    freq = np.arange(LOW, dtype=np.float32)
    wave = np.float32(2.0) * np.cos(np.float32(math.pi) * freq / np.float32(TILE))
    held = (wave[:, None] + wave[None, :]).astype(np.float32) - np.float32(4.0)
    exact = mu[:LOW, None] + mu[None, :LOW]
    delta = np.zeros((LOW, LOW))
    known = exact > 0.0
    delta[known] = exact[known] / -held[known].astype(np.float64) - 1.0
    lift = np.zeros((2 * LOW, LANES))
    lift[:LOW, :LOW] = delta
    lift[LOW:, :LOW][known] = delta[known] / exact[known]
    basis = np.zeros((TILE, LANES))
    basis[:, :LOW] = c[:LOW].T
    starts = (delta[0, :LOW] * c[:LOW, 0]) @ c[:LOW]
    ends = (delta[0, :LOW] * c[:LOW, -1]) @ c[:LOW]
    after = lambda g: np.cumsum(g[::-1])[::-1] - g
    edges = np.zeros((8, TILE))
    edges[:4] = np.stack([starts, ends, -TURN * after(starts), -TURN * after(ends)]) / TILE
    low = dict(
        lift=lift.astype(np.float32),
        basis=np.concatenate([across, basis], 1).astype(ml_dtypes.bfloat16),
        across=across.astype(ml_dtypes.bfloat16),
        waves=c[:LOW, : TILE // 2].astype(np.float32).reshape(-1),
        edges=edges.astype(np.float32),
        steps=edges[:4].astype(np.float32).reshape(-1),
    )
    twice = lambda v: np.concatenate([v, v], 1).astype(np.float32)
    weights = weights.reshape(TILE // 2, 2, LANES).swapaxes(0, 1).astype(np.float32)
    return forward, backward, weights, twice(middle), low


def turns(u):
    return (u + MAGIC) - MAGIC


def lanes(shape):
    return lax.broadcasted_iota(jnp.int32, shape, 1)


def rows_of(shape):
    return lax.broadcasted_iota(jnp.int32, shape, 0)


def span_copies(x_ref, xv, sems, start, size, t):
    view = xv.reshape(PARTS, ROWS, PITCH, LANES)
    copies = []
    for part in range(PARTS):
        ends = (
            x_ref.at[:, pl.ds(start, size), pl.ds(part * LANES, LANES)],
            view.at[part, :, pl.ds(start, size), :],
        )
        copies.append(pltpu.make_async_copy(*ends, sems.at[t * PARTS + part]))
    return copies


def side_start(t, side):
    start = CHUNK * t if side == 0 else TILE - CHUNK * (t + 1)
    return start if isinstance(start, int) else pl.multiple_of(start, CHUNK)


def field_copies(x_ref, xv, sems, t, out=False):
    view = xv.reshape(PARTS, ROWS, PITCH, LANES)
    copies = []
    for side in range(2):
        for part in range(PARTS):
            span = pl.ds(side_start(t, side), CHUNK)
            ends = (x_ref.at[:, span, pl.ds(part * LANES, LANES)], view.at[part, :, span, :])
            sem = sems.at[(2 * t + side) * PARTS + part]
            copies.append(pltpu.make_async_copy(*(ends[::-1] if out else ends), sem))
    return copies


def span_copy(x_ref, xv, sem, start, size, out=False):
    first = start * PARTS // SUB if isinstance(start, int) else start // SUB * PARTS
    blocks = pl.ds(first, size * PARTS // SUB)
    ends = (x_ref.at[:, blocks], xv.at[:, blocks])
    return pltpu.make_async_copy(*(ends[::-1] if out else ends), sem)


def block_copies(x_ref, xv, sems, t, out=False):
    return [
        span_copy(x_ref, xv, sems.at[2 * t + side], side_start(t, side), CHUNK, out)
        for side in range(2)
    ]


def row_set(xv, base, i, part):
    start = base * PARTS + (i // SUB * PARTS + part) * SUB + i % SUB
    return xv.reshape(ROWS * BLOCK_PITCH * SUB, LANES), pl.ds(start, ROWS, stride=BLOCK_PITCH * SUB)


def row_copies(y_ref, yb, sems, t, out=False):
    copies = []
    for side in range(2):
        span = pl.ds(side_start(t, side) * ROWS, CHUNK * ROWS)
        ends = (y_ref.at[span, :], yb.at[span, :])
        copies.append(pltpu.make_async_copy(*(ends[::-1] if out else ends), sems.at[2 * t + side]))
    return copies


def start_all(copies):
    for copy in copies:
        copy.start()


def wait_all(copies):
    for copy in copies:
        copy.wait()


def rows_at(xv, a, parts=PARTS):
    where = pl.ds(a, ROWS, stride=PITCH)
    return jnp.concatenate([xv[part, where, :] for part in range(parts)], 1)


def counts_kernel(
    x_ref, edge_hbm, step_hbm, across_hbm, all_ref, loc_ref,
    msg_ref, xv, edge_ref, step_ref, across_ref, sems, table_sems
):
    tables_in = [
        pltpu.make_async_copy(step_hbm, step_ref, table_sems.at[0]),
        pltpu.make_async_copy(edge_hbm, edge_ref, table_sems.at[1]),
        pltpu.make_async_copy(across_hbm, across_ref, table_sems.at[2]),
    ]
    for copy in tables_in:
        copy.start()
    span = TILE // LOADS
    for t in range(LOADS):
        start_all(span_copies(x_ref, xv, sems, t * span, span, t))
    for copy in tables_in:
        copy.wait()
    lane128 = lanes((ROWS, 128))
    zero = jnp.zeros((ROWS, WIDTH), jnp.float32)
    half = jnp.zeros((ROWS, TILE), jnp.float32)
    acc_b, acc_a, acc_aw, acc_z = zero, half, half, zero
    acc_s, acc_e = half, half
    msg_ref[...] = jnp.zeros((MSG, LANES), jnp.float32)

    def chunk(t, carry):
        acc_b, acc_m, acc_a, acc_aw, acc_z, acc_s, acc_e, prev = carry

        wait_all(span_copies(x_ref, xv, sems, pl.multiple_of(t * span, span), span, t))
        half = t // (LOADS // 2)
        near = pl.ds(pl.multiple_of(8 * half, 8), 8)
        far = pl.ds(pl.multiple_of(16 + 8 * half, 8), 8)
        first, last = msg_ref[near, :], msg_ref[far, :]
        own = []
        for i in range(span):
            a = t * span + i
            z = rows_at(xv, a)
            u = z * PER_TURN
            own.append(u)
            if i == 0:
                prev = jnp.where(t == 0, u[:, :TILE], prev)
            ka = turns(u[:, :TILE] - prev)
            edge = pltpu.roll(u[:, TILE - LANES : TILE], 1, axis=1)
            acc_m = acc_m + turns(u[:, TILE : TILE + LANES] - edge)
            here = lane128 == (a % LANES)
            first = jnp.where(here, z[:, 0:1], first)
            last = jnp.where(here, z[:, WIDTH - 1 :], last)
            weight = (TILE - a).astype(jnp.float32)
            above = jnp.maximum(a - 1, 0)
            left = z[:, :TILE]
            acc_s = acc_s + (step_ref[a] * left + step_ref[2 * TILE + above] * ka)
            acc_e = acc_e + (step_ref[TILE + a] * left + step_ref[3 * TILE + above] * ka)
            acc_a = acc_a + ka
            acc_aw = acc_aw + weight * ka
            acc_z = acc_z + z
            prev = u[:, :TILE]
        msg_ref[near, :] = first
        msg_ref[far, :] = last
        own = jnp.concatenate(own, 0).astype(jnp.bfloat16)
        own = jnp.concatenate([own[:, :TILE], own[:, TILE:]], 0)
        kb = turns(jnp.dot(own, across_ref[...], preferred_element_type=jnp.float32))
        for i in range(span):
            pair = [kb[(c * span + i) * ROWS : (c * span + i + 1) * ROWS] for c in range(COLS)]
            acc_b = acc_b + jnp.concatenate(pair, 1)
        return acc_b, acc_m, acc_a, acc_aw, acc_z, acc_s, acc_e, prev

    start = (acc_b, jnp.zeros((ROWS, LANES), jnp.float32), acc_a, acc_aw, acc_z, acc_s, acc_e, half)
    acc_b, acc_m, acc_a, acc_aw, acc_z, acc_s, acc_e, _ = lax.fori_loop(0, LOADS, chunk, start
    )
    z_top = rows_at(xv, 0, 2)
    z_bottom = rows_at(xv, TILE - 1, 2)
    below = pltpu.roll(z_top, ROWS - 1, axis=0)
    seam = turns((below - z_bottom) * PER_TURN)
    seam = jnp.where(rows_of((ROWS, TILE)) == ROWS - 1, 0.0, seam)
    acc_a = acc_a + seam
    falling = (TILE - 1 - lanes((ROWS, TILE))).astype(jnp.float32) * (1.0 / TILE**2)
    total = lambda v: jnp.sum(v, axis=1, keepdims=True)
    edge = lambda k: edge_ref[k : k + 1, :]
    totals, means = [], []
    for c in range(COLS):
        k, z = (v[:, c * TILE : (c + 1) * TILE] for v in (acc_b, acc_z))
        begin = total(z * edge(0) + k * edge(2))
        end = total(z * edge(1) + k * edge(3))
        totals.append(total(k) * (1.0 / TILE) - (end - begin) * PER_TURN)
        means.append(total(k * falling) + begin * PER_TURN)
    totals[0] = totals[0] + acc_m[:, 0:1] * (1.0 / TILE)
    first_total, whole_total = totals[0], totals[0] + totals[1]
    begin, end = total(acc_s), total(acc_e)
    down_total = total(acc_a) * (1.0 / TILE) - (end - begin) * PER_TURN
    down_mean = total(acc_aw) * (1.0 / TILE**2) + begin * PER_TURN
    phase_mean = total(acc_z[:, :TILE]) * (1.0 / TILE**2)
    row = rows_of((ROWS, 128))
    edge = jnp.where(row == 0, z_top[0:1, :128], 0.0)
    edge = jnp.where(row == 1, z_top[0:1, 128:], edge)
    edge = jnp.where(row == 2, z_bottom[ROWS - 1 :, :128], edge)
    edge = jnp.where(row == 3, z_bottom[ROWS - 1 :, 128:], edge)
    msg_ref[pl.ds(32, 8), :] = edge
    values = [whole_total, means[0], down_total, down_mean, phase_mean]
    packed = jnp.zeros((ROWS, 128), jnp.float32)
    for index, value in enumerate(values):
        packed = jnp.where(lane128 == index, value, packed)
    msg_ref[pl.ds(40, 8), :] = packed
    packed = jnp.zeros((ROWS, 128), jnp.float32)
    for index, value in enumerate([first_total, means[0], means[1]]):
        packed = jnp.where(lane128 == index, value, packed)
    loc_ref[...] = packed
    for peer in range(all_ref.shape[0]):
        all_ref[peer] = msg_ref[...]


def across_kernel(got_ref, loc_ref, down_ref, part_ref):
    me = lax.axis_index("col")
    peers = got_ref.shape[0]
    before = jnp.zeros((ROWS, 1), jnp.float32)
    for peer in range(peers - 1):
        border = jnp.zeros((ROWS, 128), jnp.float32)
        for part in range(2):
            right = got_ref[peer + 1, pl.ds(8 * part, 8), :]
            left = got_ref[peer, pl.ds(16 + 8 * part, 8), :]
            border = border + turns((right - left) * PER_TURN)
        crossed = jnp.sum(border, axis=1, keepdims=True) * (1.0 / TILE)
        both = got_ref[peer, pl.ds(40, 8), 0:1] + crossed
        before = before + jnp.where(peer < me, both, 0.0)
    start = got_ref[0, pl.ds(40, 8), :]
    edge = got_ref[0, pl.ds(32, 8), :]
    loc = loc_ref[...]
    lane = lanes((ROWS, 128))
    row = rows_of((ROWS, 128))
    down = start[:, 2:3]
    down_sum = jnp.sum(down, axis=0, keepdims=True)
    info = jnp.where(lane == 0, down_sum, 0.0)
    info = jnp.where(lane == 1, start[0:1, 3:4], info)
    info = jnp.where(lane == 2, start[0:1, 4:5], info)
    info = jnp.where(row == 4, info, edge)
    for peer in range(down_ref.shape[0]):
        down_ref[peer] = info
    here = jnp.zeros((ROWS, 1), jnp.float32)
    for index in range(ROWS - 1):
        here = here + jnp.where(rows_of((ROWS, 1)) > index, down[index : index + 1, :], 0.0)
    shared = before + here - start[:, 1:2] + start[:, 3:4]
    one = shared + loc[:, 1:2]
    two = shared + loc[:, 0:1] + loc[:, 2:3]
    part_ref[...] = jnp.where(lane == 0, one, jnp.where(lane == 1, two, 0.0))


def at(a):
    return pl.ds(pl.multiple_of(a * ROWS, ROWS), ROWS)


def weight(w_ref, a):
    pair = [jnp.broadcast_to(w_ref[part, pl.ds(a, 1), :], (ROWS, LANES)) for part in range(2)]
    return jnp.concatenate(pair * COLS, 1)


def narrow(v):
    return jnp.concatenate([v[:, c * TILE : c * TILE + LANES] for c in range(COLS)], 1)


def forward_kernel(
    x_ref, fwd_ref, w_ref, mid_ref, lift_ref, basis_ref, wave_ref, y_ref, ends_ref,
    xv, yb, in_sems, out_sems
):
    for t in range(STEPS):
        start_all(field_copies(x_ref, xv, in_sems, t))
    def loaded(a):
        return rows_at(xv, a) * PER_TURN

    def sources(start):
        u = loaded(jnp.maximum(start - 1, 0))
        here = loaded(start)
        above = turns(here - u)
        out, own = [], []
        for i in range(CHUNK):
            own.append(here)
            after = loaded(jnp.minimum(start + i + 1, TILE - 1))
            below = turns(after - here)
            out.append(below - above)
            here, above = after, below
        return [jnp.concatenate(v, 0).astype(jnp.bfloat16) for v in (out, own)]

    def wave(p, a):
        return wave_ref[p * (TILE // 2) + a]

    def gather_low(low, a, top, bottom):
        even, odd = top + bottom, top - bottom
        return (
            low[0] + even,
            low[1] + wave(1, a) * odd,
            low[2] + wave(2, a) * even,
            low[3] + wave(3, a) * odd,
        )

    def transform(t, low):
        top, own_top = sources(t * CHUNK)
        bottom, own_bottom = sources(TILE - CHUNK * (t + 1))
        stack = lambda u, v: jnp.concatenate([u[:, :TILE], u[:, TILE:], v[:, :TILE], v[:, TILE:]], 0)
        left = stack(own_top, own_bottom)
        both = jnp.dot(left, basis_ref[...], preferred_element_type=jnp.float32)
        kb, own = turns(both[:, :TILE]).astype(jnp.bfloat16), both[:, TILE:]
        piece = lambda k, i: own[(k * CHUNK + i) * ROWS : (k * CHUNK + i + 1) * ROWS]
        for i in range(CHUNK):
            pair = [
                jnp.concatenate([piece(2 * side, j), piece(2 * side + 1, j)], 1)
                for side, j in ((0, i), (1, CHUNK - 1 - i))
            ]
            low = gather_low(low, t * CHUNK + i, *pair)
        left = stack(top, bottom)
        left = jnp.concatenate([left, left, kb, kb], 1)
        y = jnp.dot(left, fwd_ref[...], preferred_element_type=jnp.float32)
        size = CHUNK * ROWS
        for side in range(2):
            start = (t * CHUNK if side == 0 else TILE - CHUNK * (t + 1)) * ROWS
            start = pl.multiple_of(start, size)
            for c in range(COLS):
                piece = y[(2 * side + c) * size : (2 * side + c + 1) * size]
                yb[pl.ds(start, size), c * TILE : (c + 1) * TILE] = piece
        return low

    def eliminate(t, carry):
        top, bottom, low = carry
        for i in range(CHUNK):
            a = t * CHUNK + i
            scale = weight(w_ref, jnp.maximum(a - 1, 0))
            own_top, own_bottom = yb[at(a), :], yb[at(TILE - 1 - a), :]
            low = gather_low(low, a, narrow(own_top), narrow(own_bottom))
            top = own_top + scale * top
            bottom = own_bottom + scale * bottom
            yb[at(a), :] = top
            yb[at(TILE - 1 - a), :] = bottom
        return top, bottom, low

    zero = jnp.zeros((ROWS, WIDTH), jnp.float32)
    none = (jnp.zeros((ROWS, COLS * LANES), jnp.float32),) * LOW
    for t in range(2):
        wait_all(field_copies(x_ref, xv, in_sems, t))
    low_z = transform(0, none)

    def forward(t, carry):
        carry, low_z = carry

        @pl.when(t + 1 < STEPS)
        def _():
            wait_all(field_copies(x_ref, xv, in_sems, t + 1))

        carry = eliminate(t - 1, carry)
        low_z = transform(t, low_z)
        start_all(row_copies(y_ref, yb, out_sems, t - 1, out=True))
        return carry, low_z

    carry, low_z = lax.fori_loop(1, STEPS, forward, ((zero, zero, none), low_z))
    top, bottom, low_y = eliminate(STEPS - 1, carry)
    start_all(row_copies(y_ref, yb, out_sems, STEPS - 1, out=True))
    lift = []
    for p in range(LOW):
        rows = [
            jnp.concatenate([lift_ref[k : k + 1, :]] * COLS, 1) for k in (p, LOW + p)
        ]
        lift.append(rows[0] * low_z[p] + rows[1] * low_y[p])
    lift[0] = lift[0] * (1.0 / TILE)
    even = mid_ref[0:1, :] * (top + bottom)
    odd = mid_ref[1:2, :] * (top - bottom)
    ends_ref[0:ROWS, :] = even + odd
    ends_ref[ROWS : 2 * ROWS, :] = even - odd
    for p in range(LOW):
        for c in range(COLS):
            ends_ref[(2 + p) * ROWS : (3 + p) * ROWS, c * TILE : c * TILE + LANES] = lift[p][
                :, c * LANES : (c + 1) * LANES
            ]
    for t in range(STEPS):
        wait_all(row_copies(y_ref, yb, out_sems, t, out=True))


def backward_kernel(
    x_ref, y_ref, ends_ref, bwd_ref, w_ref, wave_ref, p_ref, sum_ref,
    xv, yb, pv, even_ref, odd_ref, x_sems, y_sems, out_sems
):
    for t in reversed(range(STEPS)):
        start_all(row_copies(y_ref, yb, y_sems, t))
        start_all(block_copies(x_ref, xv, x_sems, t))
    def wave(p, a):
        return wave_ref[p * (TILE // 2) + a]

    mid_top, mid_bottom = (ends_ref[k * ROWS : (k + 1) * ROWS, :] for k in range(2))
    lift = [narrow(ends_ref[(2 + p) * ROWS : (3 + p) * ROWS, :]) for p in range(LOW)]

    def substitute(t, carry, to_ref):
        top, bottom, total = carry
        for i in range(CHUNK):
            a = t * CHUNK + (CHUNK - 1 - i)
            scale = weight(w_ref, a)
            top = scale * (yb[at(a), :] + top)
            bottom = scale * (yb[at(TILE - 1 - a), :] + bottom)
            even = lift[0] + wave(2, a) * lift[2]
            odd = wave(1, a) * lift[1] + wave(3, a) * lift[3]
            for low, value, row in ((even + odd, top, CHUNK - 1 - i), (even - odd, bottom, CHUNK + i)):
                for part in range(PARTS):
                    piece = value[:, part * LANES : (part + 1) * LANES]
                    if part % 2 == 0:
                        piece = piece + low[:, part // 2 * LANES : (part // 2 + 1) * LANES]
                    rows = slice(row * ROWS, (row + 1) * ROWS)
                    to_ref[rows, part * LANES : (part + 1) * LANES] = piece
            total = total + narrow(top + bottom)
        return top, bottom, total

    def restore(t, from_ref):
        size = CHUNK * ROWS
        pieces, starts = [], []
        for side in range(2):
            starts.append(t * CHUNK if side == 0 else TILE - CHUNK * (t + 1))
            for c in range(COLS):
                rows = slice(side * size, (side + 1) * size)
                pieces.append(from_ref[rows, c * TILE : (c + 1) * TILE])
        value = jnp.concatenate(pieces, 0)
        high = value.astype(jnp.bfloat16)
        low = (value - high.astype(jnp.float32)).astype(jnp.bfloat16)
        left = jnp.concatenate([high, low, high], 1)
        y = jnp.dot(left, bwd_ref[...], preferred_element_type=jnp.float32)
        for side in range(2):
            for i in range(CHUNK):
                for part in range(PARTS):
                    from_row = (2 * side + part // 2) * size + i * ROWS
                    from_lane = (part % 2) * LANES
                    piece = y[from_row : from_row + ROWS, from_lane : from_lane + LANES]
                    flat, rows = row_set(xv, starts[side], i, part)
                    moved, _ = row_set(pv, starts[side], i, part)
                    moved[rows, :] = flat[rows, :] + piece

    odd_ref[...] = jnp.zeros(odd_ref.shape, jnp.float32)

    def backward(j, carry):
        t = STEPS - 1 - 2 * j
        for k in range(2):
            wait_all(row_copies(y_ref, yb, y_sems, t - k))
            wait_all(block_copies(x_ref, xv, x_sems, t - k))
        carry = substitute(t, carry, even_ref)
        restore(jnp.minimum(t + 1, STEPS - 1), odd_ref)
        carry = substitute(t - 1, carry, odd_ref)
        restore(t, even_ref)

        @pl.when(j > 0)
        def _():
            start_all(block_copies(p_ref, pv, out_sems, t + 1, out=True))

        start_all(block_copies(p_ref, pv, out_sems, t, out=True))
        return carry

    begin = (mid_bottom, mid_top, jnp.zeros((ROWS, COLS * LANES), jnp.float32))
    _, _, total = lax.fori_loop(0, STEPS // 2, backward, begin)
    restore(0, odd_ref)
    start_all(block_copies(p_ref, pv, out_sems, 0, out=True))
    sum_ref[...] = total
    for t in range(STEPS):
        wait_all(block_copies(p_ref, pv, out_sems, t, out=True))


def finish_kernel(p_ref, sum_ref, part_ref, down_ref, out_ref, stage, in_sems, out_sems):
    def block(row, out):
        rows = stage.at[row]
        ends = (rows, out_ref.at[row]) if out else (p_ref.at[row], rows)
        return pltpu.make_async_copy(*ends, (out_sems if out else in_sems).at[row])

    for row in range(ROWS):
        block(row, False).start()
    me = lax.axis_index("row")
    peers = down_ref.shape[0]
    before = jnp.zeros((1, 1), jnp.float32)
    for peer in range(peers - 1):
        border = turns((down_ref[peer + 1, 0:2, :] - down_ref[peer, 2:4, :]) * PER_TURN)
        border = jnp.sum(jnp.sum(border, axis=1, keepdims=True), axis=0, keepdims=True)
        both = border * (1.0 / TILE) + down_ref[peer, 4:5, 0:1]
        before = before + jnp.where(peer < me, both, 0.0)
    shared = before - down_ref[0, 4:5, 1:2]
    mean = down_ref[0, 4:5, 2:3]
    shift = []
    for c in range(COLS):
        level = sum_ref[:, c * LANES : c * LANES + 1] * (1.0 / (16.0 * TILE))
        value = -mean - TURN * (part_ref[:, c : c + 1] + shared + level)
        shift.append(jnp.broadcast_to(value, (ROWS, LANES)))
    for row in range(ROWS):
        block(row, False).wait()
        for part in range(PARTS):
            view = stage.reshape(ROWS, BLOCKS // PARTS, PARTS, SUB, LANES).at[row, :, part]
            view[...] = view[...] + shift[part // 2][row : row + 1, :][None]
        block(row, True).start()
    for row in range(ROWS):
        block(row, True).wait()


VMEM = pl.BlockSpec(memory_space=pltpu.VMEM)
HBM = pl.BlockSpec(memory_space=pltpu.HBM)
PIECE = pltpu.VMEM((2 * CHUNK * ROWS, WIDTH), jnp.float32)
BLOCK_FIELD = pltpu.VMEM((ROWS, BLOCK_PITCH, SUB, LANES), jnp.float32)
FIELD = pltpu.VMEM((PARTS, ROWS * PITCH, LANES), jnp.float32)
SMEM = pl.BlockSpec(memory_space=pltpu.SMEM)


def f32(*shape):
    return jax.ShapeDtypeStruct(shape, jnp.float32)


def in_hbm(x):
    return pltpu.with_memory_space_constraint(x, pltpu.HBM)


def to_all(x, axis):
    return lax.all_to_all(x, axis, 0, 0, tiled=True)


def per_device(phase):
    *big, low = tables()
    forward, backward, weights, middle = (jnp.asarray(t) for t in big)
    low = {k: jnp.asarray(v) for k, v in low.items()}
    blocks = phase.reshape(ROWS, TILE // SUB, SUB, PARTS, LANES).swapaxes(2, 3)
    blocks = blocks.reshape(ROWS, BLOCKS, SUB, LANES)
    grid = in_hbm(phase.reshape(ROWS, TILE, WIDTH))
    peers = {axis: lax.axis_size(axis) for axis in ("row", "col")}
    msg, loc = pl.pallas_call(
        counts_kernel,
        out_shape=(
            f32(peers["col"], MSG, LANES),
            f32(ROWS, LANES),
        ),
        in_specs=[HBM] * 4,
        out_specs=(VMEM,) * 2,
        scratch_shapes=[
            pltpu.VMEM((MSG, LANES), jnp.float32),
            FIELD,
            pltpu.VMEM((8, TILE), jnp.float32),
            pltpu.SMEM((4 * TILE,), jnp.float32),
            pltpu.VMEM((TILE, TILE), jnp.bfloat16),
            pltpu.SemaphoreType.DMA((LOADS * PARTS,)),
            pltpu.SemaphoreType.DMA((3,)),
        ],
        compiler_params=pltpu.CompilerParams(vmem_limit_bytes=8 << 20),
        cost_estimate=pl.CostEstimate(flops=1 << 30, bytes_accessed=4 << 20, transcendentals=0),
        name="counts",
    )(grid, in_hbm(low["edges"]), in_hbm(low["steps"]), in_hbm(low["across"]))
    got = to_all(msg, "col")
    yb, ends = pl.pallas_call(
        forward_kernel,
        out_shape=(pltpu.HBM((ROWS * TILE, WIDTH), jnp.float32), f32((2 + LOW) * ROWS, WIDTH)),
        in_specs=[HBM] + [VMEM] * 5 + [SMEM],
        out_specs=(HBM, VMEM),
        scratch_shapes=[
            pltpu.VMEM((PARTS, ROWS * PITCH, LANES), jnp.float32),
            pltpu.VMEM((ROWS * TILE, WIDTH), jnp.float32),
            pltpu.SemaphoreType.DMA((2 * STEPS * PARTS,)),
            pltpu.SemaphoreType.DMA((2 * STEPS,)),
        ],
        compiler_params=pltpu.CompilerParams(vmem_limit_bytes=12 << 20),
        cost_estimate=pl.CostEstimate(flops=8 << 30, bytes_accessed=8 << 20, transcendentals=0),
        name="ahead",
    )(grid, forward, weights, middle, low["lift"], low["basis"], low["waves"])
    down, part = pl.pallas_call(
        across_kernel,
        out_shape=(f32(peers["row"], ROWS, LANES), f32(ROWS, LANES)),
        in_specs=[VMEM, VMEM],
        out_specs=(VMEM, VMEM),
        compiler_params=pltpu.CompilerParams(vmem_limit_bytes=4 << 20),
        name="across",
    )(got, loc)
    downs = to_all(down, "row")
    p, total = pl.pallas_call(
        backward_kernel,
        out_shape=(pltpu.HBM((ROWS, BLOCKS, SUB, LANES), jnp.float32), f32(ROWS, COLS * LANES)),
        in_specs=[HBM, HBM] + [VMEM] * 3 + [SMEM],
        out_specs=(HBM, VMEM),
        scratch_shapes=[
            BLOCK_FIELD,
            pltpu.VMEM((ROWS * TILE, WIDTH), jnp.float32),
            BLOCK_FIELD,
            PIECE,
            PIECE,
            pltpu.SemaphoreType.DMA((2 * STEPS,)),
            pltpu.SemaphoreType.DMA((2 * STEPS,)),
            pltpu.SemaphoreType.DMA((2 * STEPS,)),
        ],
        compiler_params=pltpu.CompilerParams(vmem_limit_bytes=24 << 20),
        cost_estimate=pl.CostEstimate(flops=8 << 30, bytes_accessed=8 << 20, transcendentals=0),
        name="back",
    )(in_hbm(blocks), in_hbm(yb), ends, backward, weights, low["waves"])
    out = pl.pallas_call(
        finish_kernel,
        out_shape=f32(ROWS, BLOCKS, SUB, LANES),
        in_specs=[HBM, VMEM, VMEM, VMEM],
        out_specs=HBM,
        scratch_shapes=[
            pltpu.VMEM((ROWS, BLOCKS, SUB, LANES), jnp.float32),
            pltpu.SemaphoreType.DMA((ROWS,)),
            pltpu.SemaphoreType.DMA((ROWS,)),
        ],
        compiler_params=pltpu.CompilerParams(vmem_limit_bytes=8 << 20),
        name="finish",
    )(in_hbm(p), total, part, downs)
    blocks = out.reshape(ROWS, TILE // SUB, PARTS, SUB, LANES).swapaxes(2, 3)
    return blocks.reshape(phase.shape)


def solution(mesh):
    return jax.shard_map(
        per_device, mesh=mesh, in_specs=(P("row", "col"),), out_specs=P("row", "col"), check_vma=False
    )
```

```python
import math

import jax
import jax.numpy as jnp
import ml_dtypes
import numpy as np
from jax import lax
from jax.experimental import pallas as pl
from jax.experimental.pallas import tpu as pltpu
from jax.sharding import PartitionSpec as P

TILE = 256
TURN = 2.0 * math.pi
PER_TURN = 1.0 / TURN
MAGIC = 1.5 * 2.0**23
ROWS = 8
COLS = 2
WIDTH = COLS * TILE
LANES = 128
PARTS = WIDTH // LANES
PITCH = TILE + 8
SUB = 8
BLOCKS = TILE // SUB * PARTS
BLOCK_PITCH = BLOCKS + 1
LOADS = 4
CHUNK = 16
STEPS = TILE // (2 * CHUNK)
FORE = 32
FORE_STEPS = TILE // (2 * FORE)
MSG = 48
LOW = 4


def split_terms(table, terms):
    parts, rest = [], np.asarray(table, np.float64)
    for _ in range(terms):
        part = rest.astype(ml_dtypes.bfloat16)
        parts.append(part)
        rest = rest - part.astype(np.float64)
    return parts


def tables():
    q = np.arange(TILE, dtype=np.float64)
    c = np.cos(math.pi * q[:, None] * (2.0 * q[None, :] + 1.0) / (2.0 * TILE))
    c *= math.sqrt(2.0 / TILE)
    c[0] *= math.sqrt(0.5)
    step = np.zeros_like(c.T)
    step[:-1] = c.T[:-1] - c.T[1:]
    forward = np.concatenate(split_terms(c.T, 2) + split_terms(step, 2), 0)
    across = np.zeros((TILE, TILE))
    index = np.arange(TILE - 1)
    across[index + 1, index], across[index, index] = 1.0, -1.0
    high, low = split_terms(TURN * c, 2)
    backward = np.concatenate([high, high, low], 0)
    mu = 4.0 * np.sin(math.pi * q / (2.0 * TILE)) ** 2
    pivot = [1.0 + mu]
    for _ in range(TILE // 2 - 1):
        pivot.append(2.0 + mu - 1.0 / pivot[-1])
    weights = np.stack([1.0 / d for d in pivot])
    last = pivot[-1]
    even = np.zeros_like(mu)
    even[1:] = 0.5 / (last[1:] - 1.0)
    odd = 0.5 / (last + 1.0)
    middle = np.stack([even, odd])
    freq = np.arange(LOW, dtype=np.float32)
    wave = np.float32(2.0) * np.cos(np.float32(math.pi) * freq / np.float32(TILE))
    held = (wave[:, None] + wave[None, :]).astype(np.float32) - np.float32(4.0)
    exact = mu[:LOW, None] + mu[None, :LOW]
    delta = np.zeros((LOW, LOW))
    known = exact > 0.0
    delta[known] = exact[known] / -held[known].astype(np.float64) - 1.0
    lift = np.zeros((2 * LOW, LANES))
    lift[:LOW, :LOW] = delta
    lift[LOW:, :LOW][known] = delta[known] / exact[known]
    basis = np.zeros((TILE, LANES))
    basis[:, :LOW] = c[:LOW].T
    starts = (delta[0, :LOW] * c[:LOW, 0]) @ c[:LOW]
    ends = (delta[0, :LOW] * c[:LOW, -1]) @ c[:LOW]
    after = lambda g: np.cumsum(g[::-1])[::-1] - g
    edges = np.zeros((8, TILE))
    edges[:4] = np.stack([starts, ends, -TURN * after(starts), -TURN * after(ends)]) / TILE
    low = dict(
        lift=lift.astype(np.float32),
        basis=np.concatenate([across, basis], 1).astype(ml_dtypes.bfloat16),
        across=across.astype(ml_dtypes.bfloat16),
        waves=c[:LOW, : TILE // 2].astype(np.float32).reshape(-1),
        edges=edges.astype(np.float32),
        steps=edges[:4].astype(np.float32).reshape(-1),
    )
    twice = lambda v: np.concatenate([v, v], 1).astype(np.float32)
    weights = weights.reshape(TILE // 2, 2, LANES).swapaxes(0, 1).astype(np.float32)
    return forward, backward, weights, twice(middle), low


def turns(u):
    return (u + MAGIC) - MAGIC


def lanes(shape):
    return lax.broadcasted_iota(jnp.int32, shape, 1)


def rows_of(shape):
    return lax.broadcasted_iota(jnp.int32, shape, 0)


def span_copies(x_ref, xv, sems, start, size, t):
    view = xv.reshape(PARTS, ROWS, PITCH, LANES)
    copies = []
    for part in range(PARTS):
        ends = (
            x_ref.at[:, pl.ds(start, size), pl.ds(part * LANES, LANES)],
            view.at[part, :, pl.ds(start, size), :],
        )
        copies.append(pltpu.make_async_copy(*ends, sems.at[t * PARTS + part]))
    return copies


def side_start(t, side, chunk=CHUNK):
    start = chunk * t if side == 0 else TILE - chunk * (t + 1)
    return start if isinstance(start, int) else pl.multiple_of(start, chunk)


def field_copies(x_ref, xv, sems, t):
    view = xv.reshape(PARTS, ROWS, PITCH, LANES)
    copies = []
    for side in range(2):
        for part in range(PARTS):
            span = pl.ds(side_start(t, side, FORE), FORE)
            ends = (x_ref.at[:, span, pl.ds(part * LANES, LANES)], view.at[part, :, span, :])
            copies.append(pltpu.make_async_copy(*ends, sems.at[(2 * t + side) * PARTS + part]))
    return copies


def span_copy(x_ref, xv, sem, start, size, out=False):
    first = start * PARTS // SUB if isinstance(start, int) else start // SUB * PARTS
    blocks = pl.ds(first, size * PARTS // SUB)
    ends = (x_ref.at[:, blocks], xv.at[:, blocks])
    return pltpu.make_async_copy(*(ends[::-1] if out else ends), sem)


def block_copies(x_ref, xv, sems, t, out=False):
    return [
        span_copy(x_ref, xv, sems.at[2 * t + side], side_start(t, side), CHUNK, out)
        for side in range(2)
    ]


def row_set(xv, base, i, part):
    start = base * PARTS + (i // SUB * PARTS + part) * SUB + i % SUB
    return xv.reshape(ROWS * BLOCK_PITCH * SUB, LANES), pl.ds(start, ROWS, stride=BLOCK_PITCH * SUB)


def row_copies(y_ref, yb, sems, t, out=False, chunk=CHUNK):
    copies = []
    for side in range(2):
        span = pl.ds(side_start(t, side, chunk) * ROWS, chunk * ROWS)
        ends = (y_ref.at[span, :], yb.at[span, :])
        copies.append(pltpu.make_async_copy(*(ends[::-1] if out else ends), sems.at[2 * t + side]))
    return copies


def start_all(copies):
    for copy in copies:
        copy.start()


def wait_all(copies):
    for copy in copies:
        copy.wait()


def rows_at(xv, a, parts=PARTS):
    where = pl.ds(a, ROWS, stride=PITCH)
    return jnp.concatenate([xv[part, where, :] for part in range(parts)], 1)


def counts_kernel(
    x_ref, edge_hbm, step_hbm, across_hbm, all_ref, loc_ref,
    msg_ref, xv, edge_ref, step_ref, across_ref, sems, table_sems
):
    tables_in = [
        pltpu.make_async_copy(step_hbm, step_ref, table_sems.at[0]),
        pltpu.make_async_copy(edge_hbm, edge_ref, table_sems.at[1]),
        pltpu.make_async_copy(across_hbm, across_ref, table_sems.at[2]),
    ]
    for copy in tables_in:
        copy.start()
    span = TILE // LOADS
    for t in range(LOADS):
        start_all(span_copies(x_ref, xv, sems, t * span, span, t))
    for copy in tables_in:
        copy.wait()
    lane128 = lanes((ROWS, 128))
    zero = jnp.zeros((ROWS, WIDTH), jnp.float32)
    half = jnp.zeros((ROWS, TILE), jnp.float32)
    acc_b, acc_a, acc_aw, acc_z = zero, half, half, zero
    acc_s, acc_e = half, half
    msg_ref[...] = jnp.zeros((MSG, LANES), jnp.float32)

    def chunk(t, carry):
        acc_b, acc_m, acc_a, acc_aw, acc_z, acc_s, acc_e, prev = carry

        wait_all(span_copies(x_ref, xv, sems, pl.multiple_of(t * span, span), span, t))
        half = t // (LOADS // 2)
        near = pl.ds(pl.multiple_of(8 * half, 8), 8)
        far = pl.ds(pl.multiple_of(16 + 8 * half, 8), 8)
        first, last = msg_ref[near, :], msg_ref[far, :]
        own = []
        for i in range(span):
            a = t * span + i
            z = rows_at(xv, a)
            u = z * PER_TURN
            own.append(u)
            if i == 0:
                prev = jnp.where(t == 0, u[:, :TILE], prev)
            ka = turns(u[:, :TILE] - prev)
            edge = pltpu.roll(u[:, TILE - LANES : TILE], 1, axis=1)
            acc_m = acc_m + turns(u[:, TILE : TILE + LANES] - edge)
            here = lane128 == (a % LANES)
            first = jnp.where(here, z[:, 0:1], first)
            last = jnp.where(here, z[:, WIDTH - 1 :], last)
            weight = (TILE - a).astype(jnp.float32)
            above = jnp.maximum(a - 1, 0)
            left = z[:, :TILE]
            acc_s = acc_s + (step_ref[a] * left + step_ref[2 * TILE + above] * ka)
            acc_e = acc_e + (step_ref[TILE + a] * left + step_ref[3 * TILE + above] * ka)
            acc_a = acc_a + ka
            acc_aw = acc_aw + weight * ka
            acc_z = acc_z + z
            prev = u[:, :TILE]
        msg_ref[near, :] = first
        msg_ref[far, :] = last
        own = jnp.concatenate(own, 0).astype(jnp.bfloat16)
        own = jnp.concatenate([own[:, :TILE], own[:, TILE:]], 0)
        kb = turns(jnp.dot(own, across_ref[...], preferred_element_type=jnp.float32))
        for i in range(span):
            pair = [kb[(c * span + i) * ROWS : (c * span + i + 1) * ROWS] for c in range(COLS)]
            acc_b = acc_b + jnp.concatenate(pair, 1)
        return acc_b, acc_m, acc_a, acc_aw, acc_z, acc_s, acc_e, prev

    start = (acc_b, jnp.zeros((ROWS, LANES), jnp.float32), acc_a, acc_aw, acc_z, acc_s, acc_e, half)
    acc_b, acc_m, acc_a, acc_aw, acc_z, acc_s, acc_e, _ = lax.fori_loop(0, LOADS, chunk, start
    )
    z_top = rows_at(xv, 0, 2)
    z_bottom = rows_at(xv, TILE - 1, 2)
    below = pltpu.roll(z_top, ROWS - 1, axis=0)
    seam = turns((below - z_bottom) * PER_TURN)
    seam = jnp.where(rows_of((ROWS, TILE)) == ROWS - 1, 0.0, seam)
    acc_a = acc_a + seam
    falling = (TILE - 1 - lanes((ROWS, TILE))).astype(jnp.float32) * (1.0 / TILE**2)
    total = lambda v: jnp.sum(v, axis=1, keepdims=True)
    edge = lambda k: edge_ref[k : k + 1, :]
    totals, means = [], []
    for c in range(COLS):
        k, z = (v[:, c * TILE : (c + 1) * TILE] for v in (acc_b, acc_z))
        begin = total(z * edge(0) + k * edge(2))
        end = total(z * edge(1) + k * edge(3))
        totals.append(total(k) * (1.0 / TILE) - (end - begin) * PER_TURN)
        means.append(total(k * falling) + begin * PER_TURN)
    totals[0] = totals[0] + acc_m[:, 0:1] * (1.0 / TILE)
    first_total, whole_total = totals[0], totals[0] + totals[1]
    begin, end = total(acc_s), total(acc_e)
    down_total = total(acc_a) * (1.0 / TILE) - (end - begin) * PER_TURN
    down_mean = total(acc_aw) * (1.0 / TILE**2) + begin * PER_TURN
    phase_mean = total(acc_z[:, :TILE]) * (1.0 / TILE**2)
    row = rows_of((ROWS, 128))
    edge = jnp.where(row == 0, z_top[0:1, :128], 0.0)
    edge = jnp.where(row == 1, z_top[0:1, 128:], edge)
    edge = jnp.where(row == 2, z_bottom[ROWS - 1 :, :128], edge)
    edge = jnp.where(row == 3, z_bottom[ROWS - 1 :, 128:], edge)
    msg_ref[pl.ds(32, 8), :] = edge
    values = [whole_total, means[0], down_total, down_mean, phase_mean]
    packed = jnp.zeros((ROWS, 128), jnp.float32)
    for index, value in enumerate(values):
        packed = jnp.where(lane128 == index, value, packed)
    msg_ref[pl.ds(40, 8), :] = packed
    packed = jnp.zeros((ROWS, 128), jnp.float32)
    for index, value in enumerate([first_total, means[0], means[1]]):
        packed = jnp.where(lane128 == index, value, packed)
    loc_ref[...] = packed
    for peer in range(all_ref.shape[0]):
        all_ref[peer] = msg_ref[...]


def across_kernel(got_ref, loc_ref, down_ref, part_ref):
    me = lax.axis_index("col")
    peers = got_ref.shape[0]
    before = jnp.zeros((ROWS, 1), jnp.float32)
    for peer in range(peers - 1):
        border = jnp.zeros((ROWS, 128), jnp.float32)
        for part in range(2):
            right = got_ref[peer + 1, pl.ds(8 * part, 8), :]
            left = got_ref[peer, pl.ds(16 + 8 * part, 8), :]
            border = border + turns((right - left) * PER_TURN)
        crossed = jnp.sum(border, axis=1, keepdims=True) * (1.0 / TILE)
        both = got_ref[peer, pl.ds(40, 8), 0:1] + crossed
        before = before + jnp.where(peer < me, both, 0.0)
    start = got_ref[0, pl.ds(40, 8), :]
    edge = got_ref[0, pl.ds(32, 8), :]
    loc = loc_ref[...]
    lane = lanes((ROWS, 128))
    row = rows_of((ROWS, 128))
    down = start[:, 2:3]
    down_sum = jnp.sum(down, axis=0, keepdims=True)
    info = jnp.where(lane == 0, down_sum, 0.0)
    info = jnp.where(lane == 1, start[0:1, 3:4], info)
    info = jnp.where(lane == 2, start[0:1, 4:5], info)
    info = jnp.where(row == 4, info, edge)
    for peer in range(down_ref.shape[0]):
        down_ref[peer] = info
    here = jnp.zeros((ROWS, 1), jnp.float32)
    for index in range(ROWS - 1):
        here = here + jnp.where(rows_of((ROWS, 1)) > index, down[index : index + 1, :], 0.0)
    shared = before + here - start[:, 1:2] + start[:, 3:4]
    one = shared + loc[:, 1:2]
    two = shared + loc[:, 0:1] + loc[:, 2:3]
    part_ref[...] = jnp.where(lane == 0, one, jnp.where(lane == 1, two, 0.0))


def at(a):
    return pl.ds(pl.multiple_of(a * ROWS, ROWS), ROWS)


def weight(w_ref, a):
    pair = [jnp.broadcast_to(w_ref[part, pl.ds(a, 1), :], (ROWS, LANES)) for part in range(2)]
    return jnp.concatenate(pair * COLS, 1)


def narrow(v):
    return jnp.concatenate([v[:, c * TILE : c * TILE + LANES] for c in range(COLS)], 1)


def forward_kernel(
    x_ref, fwd_ref, w_ref, mid_ref, lift_ref, basis_ref, wave_ref, y_ref, ends_ref,
    xv, yb, in_sems, out_sems
):
    for t in range(FORE_STEPS):
        start_all(field_copies(x_ref, xv, in_sems, t))
    def loaded(a):
        return rows_at(xv, a) * PER_TURN

    def sources(start):
        u = loaded(jnp.maximum(start - 1, 0))
        here = loaded(start)
        above = turns(here - u)
        out, own = [], []
        for i in range(FORE):
            own.append(here)
            after = loaded(jnp.minimum(start + i + 1, TILE - 1))
            below = turns(after - here)
            out.append(below - above)
            here, above = after, below
        return [jnp.concatenate(v, 0).astype(jnp.bfloat16) for v in (out, own)]

    def wave(p, a):
        return wave_ref[p * (TILE // 2) + a]

    def gather_low(low, a, top, bottom):
        even, odd = top + bottom, top - bottom
        return (
            low[0] + even,
            low[1] + wave(1, a) * odd,
            low[2] + wave(2, a) * even,
            low[3] + wave(3, a) * odd,
        )

    def transform(t, low):
        top, own_top = sources(t * FORE)
        bottom, own_bottom = sources(TILE - FORE * (t + 1))
        stack = lambda u, v: jnp.concatenate([u[:, :TILE], u[:, TILE:], v[:, :TILE], v[:, TILE:]], 0)
        left = stack(own_top, own_bottom)
        both = jnp.dot(left, basis_ref[...], preferred_element_type=jnp.float32)
        kb, own = turns(both[:, :TILE]).astype(jnp.bfloat16), both[:, TILE:]
        piece = lambda k, i: own[(k * FORE + i) * ROWS : (k * FORE + i + 1) * ROWS]
        for i in range(FORE):
            pair = [
                jnp.concatenate([piece(2 * side, j), piece(2 * side + 1, j)], 1)
                for side, j in ((0, i), (1, FORE - 1 - i))
            ]
            low = gather_low(low, t * FORE + i, *pair)
        left = stack(top, bottom)
        left = jnp.concatenate([left, left, kb, kb], 1)
        y = jnp.dot(left, fwd_ref[...], preferred_element_type=jnp.float32)
        size = FORE * ROWS
        for side in range(2):
            start = (t * FORE if side == 0 else TILE - FORE * (t + 1)) * ROWS
            start = pl.multiple_of(start, size)
            for c in range(COLS):
                piece = y[(2 * side + c) * size : (2 * side + c + 1) * size]
                yb[pl.ds(start, size), c * TILE : (c + 1) * TILE] = piece
        return low

    def eliminate(t, carry):
        top, bottom, low = carry
        for i in range(FORE):
            a = t * FORE + i
            scale = weight(w_ref, jnp.maximum(a - 1, 0))
            own_top, own_bottom = yb[at(a), :], yb[at(TILE - 1 - a), :]
            low = gather_low(low, a, narrow(own_top), narrow(own_bottom))
            top = own_top + scale * top
            bottom = own_bottom + scale * bottom
            yb[at(a), :] = top
            yb[at(TILE - 1 - a), :] = bottom
        return top, bottom, low

    zero = jnp.zeros((ROWS, WIDTH), jnp.float32)
    none = (jnp.zeros((ROWS, COLS * LANES), jnp.float32),) * LOW
    for t in range(2):
        wait_all(field_copies(x_ref, xv, in_sems, t))
    low_z = transform(0, none)

    def forward(t, carry):
        carry, low_z = carry

        @pl.when(t + 1 < FORE_STEPS)
        def _():
            wait_all(field_copies(x_ref, xv, in_sems, t + 1))

        carry = eliminate(t - 1, carry)
        low_z = transform(t, low_z)
        start_all(row_copies(y_ref, yb, out_sems, t - 1, out=True, chunk=FORE))
        return carry, low_z

    carry, low_z = lax.fori_loop(1, FORE_STEPS, forward, ((zero, zero, none), low_z))
    top, bottom, low_y = eliminate(FORE_STEPS - 1, carry)
    start_all(row_copies(y_ref, yb, out_sems, FORE_STEPS - 1, out=True, chunk=FORE))
    lift = []
    for p in range(LOW):
        rows = [
            jnp.concatenate([lift_ref[k : k + 1, :]] * COLS, 1) for k in (p, LOW + p)
        ]
        lift.append(rows[0] * low_z[p] + rows[1] * low_y[p])
    lift[0] = lift[0] * (1.0 / TILE)
    even = mid_ref[0:1, :] * (top + bottom)
    odd = mid_ref[1:2, :] * (top - bottom)
    ends_ref[0:ROWS, :] = even + odd
    ends_ref[ROWS : 2 * ROWS, :] = even - odd
    for p in range(LOW):
        for c in range(COLS):
            ends_ref[(2 + p) * ROWS : (3 + p) * ROWS, c * TILE : c * TILE + LANES] = lift[p][
                :, c * LANES : (c + 1) * LANES
            ]
    for t in range(FORE_STEPS):
        wait_all(row_copies(y_ref, yb, out_sems, t, out=True, chunk=FORE))


def backward_kernel(
    x_ref, y_ref, ends_ref, bwd_ref, w_ref, wave_ref, p_ref, sum_ref,
    xv, yb, pv, even_ref, odd_ref, x_sems, y_sems, out_sems
):
    for t in reversed(range(STEPS)):
        start_all(row_copies(y_ref, yb, y_sems, t))
        start_all(block_copies(x_ref, xv, x_sems, t))
    def wave(p, a):
        return wave_ref[p * (TILE // 2) + a]

    mid_top, mid_bottom = (ends_ref[k * ROWS : (k + 1) * ROWS, :] for k in range(2))
    lift = [narrow(ends_ref[(2 + p) * ROWS : (3 + p) * ROWS, :]) for p in range(LOW)]

    def substitute(t, carry, to_ref):
        top, bottom, total = carry
        for i in range(CHUNK):
            a = t * CHUNK + (CHUNK - 1 - i)
            scale = weight(w_ref, a)
            top = scale * (yb[at(a), :] + top)
            bottom = scale * (yb[at(TILE - 1 - a), :] + bottom)
            even = lift[0] + wave(2, a) * lift[2]
            odd = wave(1, a) * lift[1] + wave(3, a) * lift[3]
            for low, value, row in ((even + odd, top, CHUNK - 1 - i), (even - odd, bottom, CHUNK + i)):
                for part in range(PARTS):
                    piece = value[:, part * LANES : (part + 1) * LANES]
                    if part % 2 == 0:
                        piece = piece + low[:, part // 2 * LANES : (part // 2 + 1) * LANES]
                    rows = slice(row * ROWS, (row + 1) * ROWS)
                    to_ref[rows, part * LANES : (part + 1) * LANES] = piece
            total = total + narrow(top + bottom)
        return top, bottom, total

    def restore(t, from_ref):
        size = CHUNK * ROWS
        pieces, starts = [], []
        for side in range(2):
            starts.append(t * CHUNK if side == 0 else TILE - CHUNK * (t + 1))
            for c in range(COLS):
                rows = slice(side * size, (side + 1) * size)
                pieces.append(from_ref[rows, c * TILE : (c + 1) * TILE])
        value = jnp.concatenate(pieces, 0)
        high = value.astype(jnp.bfloat16)
        low = (value - high.astype(jnp.float32)).astype(jnp.bfloat16)
        left = jnp.concatenate([high, low, high], 1)
        y = jnp.dot(left, bwd_ref[...], preferred_element_type=jnp.float32)
        for side in range(2):
            for i in range(CHUNK):
                for part in range(PARTS):
                    from_row = (2 * side + part // 2) * size + i * ROWS
                    from_lane = (part % 2) * LANES
                    piece = y[from_row : from_row + ROWS, from_lane : from_lane + LANES]
                    flat, rows = row_set(xv, starts[side], i, part)
                    moved, _ = row_set(pv, starts[side], i, part)
                    moved[rows, :] = flat[rows, :] + piece

    odd_ref[...] = jnp.zeros(odd_ref.shape, jnp.float32)

    def backward(j, carry):
        t = STEPS - 1 - 2 * j
        for k in range(2):
            wait_all(row_copies(y_ref, yb, y_sems, t - k))
            wait_all(block_copies(x_ref, xv, x_sems, t - k))
        carry = substitute(t, carry, even_ref)
        restore(jnp.minimum(t + 1, STEPS - 1), odd_ref)
        carry = substitute(t - 1, carry, odd_ref)
        restore(t, even_ref)

        @pl.when(j > 0)
        def _():
            start_all(block_copies(p_ref, pv, out_sems, t + 1, out=True))

        start_all(block_copies(p_ref, pv, out_sems, t, out=True))
        return carry

    begin = (mid_bottom, mid_top, jnp.zeros((ROWS, COLS * LANES), jnp.float32))
    _, _, total = lax.fori_loop(0, STEPS // 2, backward, begin)
    restore(0, odd_ref)
    start_all(block_copies(p_ref, pv, out_sems, 0, out=True))
    sum_ref[...] = total
    for t in range(STEPS):
        wait_all(block_copies(p_ref, pv, out_sems, t, out=True))


def finish_kernel(p_ref, sum_ref, part_ref, down_ref, out_ref, stage, in_sems, out_sems):
    def block(row, out):
        rows = stage.at[row]
        ends = (rows, out_ref.at[row]) if out else (p_ref.at[row], rows)
        return pltpu.make_async_copy(*ends, (out_sems if out else in_sems).at[row])

    for row in range(ROWS):
        block(row, False).start()
    me = lax.axis_index("row")
    peers = down_ref.shape[0]
    before = jnp.zeros((1, 1), jnp.float32)
    for peer in range(peers - 1):
        border = turns((down_ref[peer + 1, 0:2, :] - down_ref[peer, 2:4, :]) * PER_TURN)
        border = jnp.sum(jnp.sum(border, axis=1, keepdims=True), axis=0, keepdims=True)
        both = border * (1.0 / TILE) + down_ref[peer, 4:5, 0:1]
        before = before + jnp.where(peer < me, both, 0.0)
    shared = before - down_ref[0, 4:5, 1:2]
    mean = down_ref[0, 4:5, 2:3]
    shift = []
    for c in range(COLS):
        level = sum_ref[:, c * LANES : c * LANES + 1] * (1.0 / (16.0 * TILE))
        value = -mean - TURN * (part_ref[:, c : c + 1] + shared + level)
        shift.append(jnp.broadcast_to(value, (ROWS, LANES)))
    for row in range(ROWS):
        block(row, False).wait()
        for part in range(PARTS):
            view = stage.reshape(ROWS, BLOCKS // PARTS, PARTS, SUB, LANES).at[row, :, part]
            view[...] = view[...] + shift[part // 2][row : row + 1, :][None]
        block(row, True).start()
    for row in range(ROWS):
        block(row, True).wait()


VMEM = pl.BlockSpec(memory_space=pltpu.VMEM)
HBM = pl.BlockSpec(memory_space=pltpu.HBM)
PIECE = pltpu.VMEM((2 * CHUNK * ROWS, WIDTH), jnp.float32)
BLOCK_FIELD = pltpu.VMEM((ROWS, BLOCK_PITCH, SUB, LANES), jnp.float32)
FIELD = pltpu.VMEM((PARTS, ROWS * PITCH, LANES), jnp.float32)
SMEM = pl.BlockSpec(memory_space=pltpu.SMEM)


def f32(*shape):
    return jax.ShapeDtypeStruct(shape, jnp.float32)


def in_hbm(x):
    return pltpu.with_memory_space_constraint(x, pltpu.HBM)


def to_all(x, axis):
    return lax.all_to_all(x, axis, 0, 0, tiled=True)


def per_device(phase):
    *big, low = tables()
    forward, backward, weights, middle = (jnp.asarray(t) for t in big)
    low = {k: jnp.asarray(v) for k, v in low.items()}
    blocks = phase.reshape(ROWS, TILE // SUB, SUB, PARTS, LANES).swapaxes(2, 3)
    blocks = blocks.reshape(ROWS, BLOCKS, SUB, LANES)
    grid = in_hbm(phase.reshape(ROWS, TILE, WIDTH))
    peers = {axis: lax.axis_size(axis) for axis in ("row", "col")}
    msg, loc = pl.pallas_call(
        counts_kernel,
        out_shape=(
            f32(peers["col"], MSG, LANES),
            f32(ROWS, LANES),
        ),
        in_specs=[HBM] * 4,
        out_specs=(VMEM,) * 2,
        scratch_shapes=[
            pltpu.VMEM((MSG, LANES), jnp.float32),
            FIELD,
            pltpu.VMEM((8, TILE), jnp.float32),
            pltpu.SMEM((4 * TILE,), jnp.float32),
            pltpu.VMEM((TILE, TILE), jnp.bfloat16),
            pltpu.SemaphoreType.DMA((LOADS * PARTS,)),
            pltpu.SemaphoreType.DMA((3,)),
        ],
        compiler_params=pltpu.CompilerParams(vmem_limit_bytes=8 << 20),
        cost_estimate=pl.CostEstimate(flops=1 << 30, bytes_accessed=4 << 20, transcendentals=0),
        name="counts",
    )(grid, in_hbm(low["edges"]), in_hbm(low["steps"]), in_hbm(low["across"]))
    got = to_all(msg, "col")
    yb, ends = pl.pallas_call(
        forward_kernel,
        out_shape=(pltpu.HBM((ROWS * TILE, WIDTH), jnp.float32), f32((2 + LOW) * ROWS, WIDTH)),
        in_specs=[HBM] + [VMEM] * 5 + [SMEM],
        out_specs=(HBM, VMEM),
        scratch_shapes=[
            pltpu.VMEM((PARTS, ROWS * PITCH, LANES), jnp.float32),
            pltpu.VMEM((ROWS * TILE, WIDTH), jnp.float32),
            pltpu.SemaphoreType.DMA((2 * FORE_STEPS * PARTS,)),
            pltpu.SemaphoreType.DMA((2 * FORE_STEPS,)),
        ],
        compiler_params=pltpu.CompilerParams(vmem_limit_bytes=12 << 20),
        cost_estimate=pl.CostEstimate(flops=8 << 30, bytes_accessed=8 << 20, transcendentals=0),
        name="ahead",
    )(grid, forward, weights, middle, low["lift"], low["basis"], low["waves"])
    down, part = pl.pallas_call(
        across_kernel,
        out_shape=(f32(peers["row"], ROWS, LANES), f32(ROWS, LANES)),
        in_specs=[VMEM, VMEM],
        out_specs=(VMEM, VMEM),
        compiler_params=pltpu.CompilerParams(vmem_limit_bytes=4 << 20),
        name="across",
    )(got, loc)
    downs = to_all(down, "row")
    p, total = pl.pallas_call(
        backward_kernel,
        out_shape=(pltpu.HBM((ROWS, BLOCKS, SUB, LANES), jnp.float32), f32(ROWS, COLS * LANES)),
        in_specs=[HBM, HBM] + [VMEM] * 3 + [SMEM],
        out_specs=(HBM, VMEM),
        scratch_shapes=[
            BLOCK_FIELD,
            pltpu.VMEM((ROWS * TILE, WIDTH), jnp.float32),
            BLOCK_FIELD,
            PIECE,
            PIECE,
            pltpu.SemaphoreType.DMA((2 * STEPS,)),
            pltpu.SemaphoreType.DMA((2 * STEPS,)),
            pltpu.SemaphoreType.DMA((2 * STEPS,)),
        ],
        compiler_params=pltpu.CompilerParams(vmem_limit_bytes=24 << 20),
        cost_estimate=pl.CostEstimate(flops=8 << 30, bytes_accessed=8 << 20, transcendentals=0),
        name="back",
    )(in_hbm(blocks), in_hbm(yb), ends, backward, weights, low["waves"])
    out = pl.pallas_call(
        finish_kernel,
        out_shape=f32(ROWS, BLOCKS, SUB, LANES),
        in_specs=[HBM, VMEM, VMEM, VMEM],
        out_specs=HBM,
        scratch_shapes=[
            pltpu.VMEM((ROWS, BLOCKS, SUB, LANES), jnp.float32),
            pltpu.SemaphoreType.DMA((ROWS,)),
            pltpu.SemaphoreType.DMA((ROWS,)),
        ],
        compiler_params=pltpu.CompilerParams(vmem_limit_bytes=8 << 20),
        name="finish",
    )(in_hbm(p), total, part, downs)
    blocks = out.reshape(ROWS, TILE // SUB, PARTS, SUB, LANES).swapaxes(2, 3)
    return blocks.reshape(phase.shape)


def solution(mesh):
    return jax.shard_map(
        per_device, mesh=mesh, in_specs=(P("row", "col"),), out_specs=P("row", "col"), check_vma=False
    )
```
